256 devices in a mesh: ctx: 16 (over y, z_hi), head: 16 (over x, z_lo, core).
Axes of the slice: x: 4, y: 4, z: 8 (z_hi: 4, z_lo: 2; z = z_hi * 2 + z_lo), core: 2. Of those that a mesh axis runs over, the one named last changes fastest.
Arguments:
- queries: bfloat16 [16384, 4096], P('ctx', 'head'), parts along dimension 1, may hold values from -15 to 15
- key_rows: bfloat16 [16384, 2048], P('ctx', 'head'), parts along dimension 1, may hold values from -6 to 6
- value_rows: bfloat16 [16384, 2048], P('ctx', 'head'), parts along dimension 1, may hold values from -16 to 16
- block_order: int32 [16], replicated, may hold values from 0 to 15, each once
Outputs:
- attended: bfloat16 [16384, 4096], P('ctx', 'head'), parts along dimension 1
The draws below stay inside these ranges and needn't reach their ends.
There are 16 independent parts, one for each index of `head`. The reference program is written for one: setup_inputs(seed, part) draws one part's arguments, and reference() takes and returns one part's arrays. A program takes and returns all parts, laid end to end along the dimension named above; an argument that names none is the same for every part. Nothing has to cross between parts.
Inputs may be any that keep to these rules, and one draw needn't show every extreme that they name: `block_order`: each block number appears once.
All inputs are finite; a program needn't handle non-finite values.
Results may differ from the reference program's by a relative error of at most 0.0033.
Values may be sent and summed in bfloat16 or wider, within the bound.
No kernel may reach another device: no remote copies, remote signals or barrier semaphores. Data moves between devices by JAX's collectives and lax.ppermute only.
A program may use at most 128 MiB of HBM per device.

```python
import jax
import jax.numpy as jnp
from jax import lax

HD = 128
QH = 2
TOK_DEV = 1024
BLOCKS = 16
SEQ = 16384


def paired_rows(key):
    folded = jax.random.fold_in(key, 2711)
    query_key, row_key = jax.random.split(folded, 2)
    queries = jnp.clip(2.5 * jax.random.normal(query_key, (SEQ, QH * HD), jnp.float32), -15.0, 15.0)
    key_rows = jnp.clip(jax.random.normal(row_key, (SEQ, HD), jnp.float32), -6.0, 6.0)
    return (queries, key_rows)


def draw_queries(key, part):
    return paired_rows(key)[0].astype(jnp.bfloat16)


def draw_key_rows(key, part):
    return paired_rows(key)[1].astype(jnp.bfloat16)


def block_levels(rng, dims, cuts, low, top_value):
    level = 1.0
    for position, blocks in cuts:
        heights = jax.random.uniform(jax.random.fold_in(jax.random.fold_in(rng, 6), position), (blocks,), jnp.float32, low / len(cuts), top_value / len(cuts))
        level = level * jnp.repeat(jnp.exp(heights), dims[position] // blocks).reshape((-1,) + (1,) * (len(dims) - 1 - position))
    return level


def bell_draw(own_key, dims, deviation, bound, cuts=(), kind=jnp.bfloat16):
    level = block_levels(own_key, dims, cuts, -0.22, 0.18) if cuts else 1.0
    entries = jax.random.normal(own_key, dims, jnp.float32) * deviation * level
    return jnp.minimum(jnp.maximum(entries, -bound), bound).astype(kind)


def setup_inputs(seed: int = 0, part: int = 0) -> dict:
    key_list = jax.random.split(jax.random.key(seed), 5)
    part_splits = jax.random.split(jax.random.fold_in(key_list[4], part), 5)
    queries = draw_queries(jax.random.fold_in(jax.random.fold_in(key_list[4], part), 71), part)
    key_rows = draw_key_rows(jax.random.fold_in(jax.random.fold_in(key_list[4], part), 71), part)
    value_rows = bell_draw(part_splits[2], (SEQ, HD), 4.0, 16.0, ((0, 16),))
    block_order = jax.random.permutation(key_list[3], BLOCKS).astype(jnp.int32)
    return dict(queries=queries, key_rows=key_rows, value_rows=value_rows, block_order=block_order)


score_scale = 168.0 ** -0.5


def positions_of(block_order, count):
    row_ids = jnp.arange(count, dtype=jnp.int32)
    return block_order[row_ids // TOK_DEV] * TOK_DEV + row_ids % TOK_DEV


def reference(queries, key_rows, value_rows, block_order):
    key_pos = positions_of(block_order, SEQ)
    keys_wide = key_rows.astype(jnp.float32)
    values_wide = value_rows.astype(jnp.float32)

    def one_block(block_index):
        row_start = block_index * TOK_DEV
        query_block = lax.dynamic_slice_in_dim(queries, row_start, TOK_DEV, 0)
        query_block = query_block.astype(jnp.float32).reshape(TOK_DEV, QH, HD)
        query_pos = lax.dynamic_slice_in_dim(key_pos, row_start, TOK_DEV, 0)

        def key_step(carry, key_index):
            run_sum, run_max, run_total = carry
            key_start = key_index * TOK_DEV
            tile_keys = lax.dynamic_slice_in_dim(keys_wide, key_start, TOK_DEV, 0)
            tile_values = lax.dynamic_slice_in_dim(values_wide, key_start, TOK_DEV, 0)
            tile_pos = lax.dynamic_slice_in_dim(key_pos, key_start, TOK_DEV, 0)
            scores = jnp.einsum("qhd,kd->hqk", query_block, tile_keys) * score_scale
            visible = tile_pos[None, :] <= query_pos[:, None]
            scores = jnp.where(visible[None], scores, -jnp.inf)
            block_max = jnp.maximum(jnp.max(scores, axis=2), -1e30)
            weights = jnp.exp(scores - block_max[:, :, None])
            block_total = jnp.sum(weights, axis=2)
            rounded = lax.optimization_barrier(weights.astype(jnp.bfloat16)).astype(jnp.float32)
            block_sum = jnp.einsum("hqk,kd->hqd", rounded, tile_values)
            new_max = jnp.maximum(run_max, block_max)
            scale_old = jnp.exp(run_max - new_max)
            scale_new = jnp.exp(block_max - new_max)
            run_sum = run_sum * scale_old[:, :, None] + block_sum * scale_new[:, :, None]
            run_total = run_total * scale_old + block_total * scale_new
            return (run_sum, new_max, run_total), None

        start = (jnp.zeros((QH, TOK_DEV, HD), jnp.float32),
                 jnp.full((QH, TOK_DEV), -1e30, jnp.float32),
                 jnp.zeros((QH, TOK_DEV), jnp.float32))
        final, unused = lax.scan(key_step, start, jnp.arange(BLOCKS, dtype=jnp.int32))
        blended = final[0] / final[2][:, :, None]
        return blended.transpose(1, 0, 2).reshape(TOK_DEV, QH * HD).astype(jnp.bfloat16)

    outputs = lax.map(one_block, jnp.arange(BLOCKS, dtype=jnp.int32))
    return outputs.reshape(SEQ, QH * HD)
```

```python
import jax
import jax.numpy as jnp
from jax import lax
from jax.experimental import pallas as pl
from jax.experimental.pallas import tpu as pltpu
from jax.sharding import PartitionSpec as P

HD = 128
QH = 2
TOK = 1024
ROWS = HD + 8
SCALE = 168.0 ** (-0.5) * 1.4426950408889634
VMEM = pl.BlockSpec(memory_space=pltpu.VMEM)
SMEM = pl.BlockSpec(memory_space=pltpu.SMEM)
ANY = pl.BlockSpec(memory_space=pl.ANY)
F32 = jnp.float32
BF16 = jnp.bfloat16


def dot_last(a, b):
    return lax.dot_general(a, b, (((1,), (1,)), ((), ())), preferred_element_type=F32)


def dot_mid(a, b):
    return lax.dot_general(a, b, (((1,), (0,)), ((), ())), preferred_element_type=F32)


def key_mate(y, core):
    return y ^ 1 if core == 0 else (((y - 1) % 4 ^ 1) + 1) % 4


def query_mate(y, core):
    return key_mate(y, 1 - core)


def mate_perm(mate):
    return [
        ((y * 4 + z) * 16 + h, (mate(y, h % 2) * 4 + z) * 16 + h)
        for y in range(4) for z in range(4) for h in range(16)
    ]


def ring_perm(step):
    return [
        ((y * 4 + z) * 16 + h, (y * 4 + (z + step) % 4) * 16 + h)
        for y in range(4) for z in range(4) for h in range(16)
    ]


def send(array, perm):
    return lax.ppermute(array, ("ctx", "head"), perm)


def head(ref, h):
    return ref[:, h * HD:(h + 1) * HD]


def fill_values(vt, pieces):
    for piece, start in pieces:
        rows = piece.shape[0]
        vt[:HD, start:start + rows] = piece[:, HD:].T


def absorb(pieces, vt, q_ref, acc, shift):
    items = [(h, piece, start) for piece, start in pieces for h in range(QH)]

    def score(item):
        h, piece, _ = item
        return dot_last(piece[:, :HD], head(q_ref, h))

    scores = score(items[0])
    for n, (h, piece, start) in enumerate(items):
        upcoming = score(items[n + 1]) if n + 1 < len(items) else None
        weights = jnp.exp2(scores * SCALE - shift[h]).astype(BF16)
        acc[h] += dot_mid(vt[:, start:start + piece.shape[0]], weights)
        scores = upcoming


def block_at(index, offset):
    return (index & 12) | ((index + offset) & 3)


def diagonal_kernel(q_ref, kv_ref, acc, shift, vt):
    vt[HD:, :] = jnp.ones((8, TOK), BF16)
    fill_values(vt, [(kv_ref, 0)])
    keys = lax.broadcasted_iota(jnp.int32, (TOK, TOK), 0)
    rows = lax.broadcasted_iota(jnp.int32, (TOK, TOK), 1)
    for h in range(QH):
        scores = dot_last(kv_ref[:, :HD], head(q_ref, h)) * SCALE
        scores = jnp.where(keys <= rows, scores, -jnp.inf)
        shift[h] = jnp.max(scores, axis=0, keepdims=True)
        weights = jnp.exp2(scores - shift[h]).astype(BF16)
        acc[h] = dot_mid(vt[...], weights)


def diagonal(q, kv):
    return pl.pallas_call(
        diagonal_kernel,
        out_shape=[
            jax.ShapeDtypeStruct((QH, ROWS, TOK), F32),
            jax.ShapeDtypeStruct((QH, 1, TOK), F32),
        ],
        in_specs=[VMEM, VMEM],
        out_specs=[VMEM, VMEM],
        scratch_shapes=[pltpu.VMEM((ROWS, TOK), BF16)],
        compiler_params=pltpu.CompilerParams(vmem_limit_bytes=40 << 20),
        cost_estimate=pl.CostEstimate(flops=3 << 30, bytes_accessed=4 << 20, transcendentals=2 << 20),
        name="diagonal",
    )(q, kv)


def pieces_of(refs):
    grouped, n = [], 0
    while n < len(refs):
        if refs[n].shape[0] == TOK:
            grouped.append([(refs[n], 0)])
            n += 1
        else:
            grouped.append([(refs[n], 0), (refs[n + 1], TOK // 2)])
            n += 2
    return grouped


def run_units(meta, order, q_refs, q_ids, blocks, block_ids, accs, shifts, vt):
    vt[HD:, :] = jnp.ones((8, TOK), BF16)
    for pieces, (base, offset) in zip(blocks, block_ids):
        rank = order[block_at(meta[base], offset)]
        wanted = [rank < order[meta[q]] for q in q_ids]
        either = wanted[0]
        for other in wanted[1:]:
            either = jnp.logical_or(either, other)

        @pl.when(either)
        def _():
            fill_values(vt, pieces)
            for want, q_ref, acc, shift in zip(wanted, q_refs, accs, shifts):
                @pl.when(want)
                def _():
                    absorb(pieces, vt, q_ref, acc, shift)


def stage(meta, order, qs, q_ids, kvs, block_ids, states, fresh=None):
    nq, nk = len(qs), len(kvs)
    carried = [n for n in range(nq) if n != fresh]

    def kernel(*refs):
        meta_ref, order_ref = refs[:2]
        q_refs = refs[2:2 + nq]
        kv_refs = refs[2 + nq:2 + nq + nk]
        at = 2 + nq + nk
        olds = refs[at:at + 2 * len(carried)]
        at += 2 * len(carried)
        accs = refs[at:at + 2 * nq:2]
        shifts = refs[at + 1:at + 2 * nq:2]
        vt = refs[at + 2 * nq]
        for n, place in enumerate(carried):
            accs[place][...] = olds[2 * n][...]
            shifts[place][...] = olds[2 * n + 1][...]
        if fresh is not None:
            accs[fresh][...] = jnp.zeros((QH, ROWS, TOK), F32)
            for h in range(QH):
                scores = dot_last(kv_refs[0][:, :HD], head(q_refs[fresh], h))
                shifts[fresh][h] = jnp.max(scores, axis=0, keepdims=True) * SCALE
        run_units(meta_ref, order_ref, q_refs, q_ids, pieces_of(kv_refs), block_ids, accs, shifts, vt)

    old = [x for n in carried for x in states[n]]
    out = pl.pallas_call(
        kernel,
        out_shape=[
            jax.ShapeDtypeStruct((QH, ROWS, TOK), F32),
            jax.ShapeDtypeStruct((QH, 1, TOK), F32),
        ] * nq,
        in_specs=[SMEM, SMEM] + [VMEM] * (nq + nk + len(old)),
        out_specs=[VMEM] * (2 * nq),
        scratch_shapes=[pltpu.VMEM((ROWS, TOK), BF16)],
        compiler_params=pltpu.CompilerParams(vmem_limit_bytes=48 << 20),
        cost_estimate=pl.CostEstimate(
            flops=len(block_ids) * nq << 31, bytes_accessed=8 << 20, transcendentals=nq * len(block_ids) << 21
        ),
        name="stage",
    )(meta, order, *qs, *kvs, *old)
    return [tuple(out[2 * n:2 * n + 2]) for n in range(nq)]


ALL_IDS = [(b, o) for b in (0, 1) for o in (0, 3, 1, 2)]


def recompute(meta, order, q_id, q_ref, sources, acc, shift, buf, vt):
    query_rank = order[meta[q_id]]
    acc[...] = jnp.zeros((QH, ROWS, TOK), F32)
    shift[...] = jnp.full((QH, 1, TOK), -1e30, F32)

    @pl.loop(0, 8)
    def _(step):
        base = step // 4
        offset = jnp.where(step % 4 == 0, 0, jnp.where(step % 4 == 1, 3, jnp.where(step % 4 == 2, 1, 2)))
        rank = order[block_at(meta[base], offset)]

        @pl.when(rank <= query_rank)
        def _():
            for n, pieces in enumerate(sources):
                @pl.when(step == n)
                def _():
                    for piece, start in pieces:
                        pltpu.sync_copy(piece, buf.at[pl.ds(start, piece.shape[0])])
            fill_values(vt, [(buf, 0)])

            @pl.loop(0, 4)
            def _(tile):
                cols = pl.ds(pl.multiple_of(tile * 256, 256), 256)
                keys = lax.broadcasted_iota(jnp.int32, (TOK, 256), 0) + rank * TOK
                rows = lax.broadcasted_iota(jnp.int32, (TOK, 256), 1) + query_rank * TOK + tile * 256
                for h in range(QH):
                    scores = dot_last(buf[:, :HD], q_ref[cols, h * HD:(h + 1) * HD]) * SCALE
                    scores = jnp.where(keys <= rows, scores, -jnp.inf)
                    old = shift[h, :, cols]
                    new = jnp.maximum(old, jnp.max(scores, axis=0, keepdims=True))
                    weights = jnp.exp2(scores - new).astype(BF16)
                    acc[h, :, cols] = acc[h, :, cols] * jnp.exp2(old - new) + dot_mid(vt[...], weights)
                    shift[h, :, cols] = new


def last_stage(meta, order, q, q_id, kvs, block_ids, state, everything, pack):
    nk, ne = len(kvs), len(everything)

    def kernel(*refs):
        meta_ref, order_ref, q_ref = refs[:3]
        kv_refs = refs[3:3 + nk]
        old_acc, old_shift = refs[3 + nk:5 + nk]
        all_refs = refs[5 + nk:5 + nk + ne]
        if pack:
            sent, acc, shift, vt, buf = refs[5 + nk + ne:]
        else:
            acc, shift, vt, buf = refs[5 + nk + ne:]
        acc[...] = old_acc[...]
        shift[...] = old_shift[...]
        run_units(meta_ref, order_ref, [q_ref], [q_id], pieces_of(kv_refs), block_ids, [acc], [shift], vt)
        query_rank = order_ref[meta_ref[q_id]]
        active = jnp.int32(0)
        for base, offset in ALL_IDS:
            active += (order_ref[block_at(meta_ref[base], offset)] <= query_rank).astype(jnp.int32)
        totals = jnp.concatenate([acc[h, HD:HD + 1, :] for h in range(QH)], axis=0)
        fine = jnp.logical_and(totals > 2.0 ** -60, totals < 2.0 ** 100)
        faults = jnp.sum(jnp.where(fine, 0.0, 1.0))

        @pl.when(jnp.logical_and(active > 0, faults > 0.0))
        def _():
            recompute(meta_ref, order_ref, q_id, q_ref, pieces_of(all_refs), acc, shift, buf, vt)

        if pack:
            for h in range(QH):
                total = acc[h, HD:HD + 1, :]
                empty = total <= 0.0
                safe = jnp.where(empty, 1.0, total)
                sent[h * HD:(h + 1) * HD, :] = (acc[h, :HD, :] / safe).astype(BF16)
                level = jnp.where(empty, -1e30, shift[h] + jnp.log2(safe))
                first = level.astype(BF16).astype(F32)
                second = (level - first).astype(BF16).astype(F32)
                third = level - first - second
                row = lax.broadcasted_iota(jnp.int32, (8, TOK), 0)
                packed = jnp.where(row == 0, first, jnp.where(row == 1, second, third))
                sent[QH * HD + 8 * h:QH * HD + 8 * h + 8, :] = packed.astype(BF16)

    state_shapes = [((QH, ROWS, TOK), F32), ((QH, 1, TOK), F32)]
    scratch = [pltpu.VMEM((ROWS, TOK), BF16), pltpu.VMEM((TOK, 2 * HD), BF16)]
    if pack:
        out_shape = jax.ShapeDtypeStruct((QH * HD + 16, TOK), BF16)
        out_specs = VMEM
        scratch = [pltpu.VMEM(*s) for s in state_shapes] + scratch
    else:
        out_shape = [jax.ShapeDtypeStruct(*s) for s in state_shapes]
        out_specs = [VMEM, VMEM]
    return pl.pallas_call(
        kernel,
        out_shape=out_shape,
        in_specs=[SMEM, SMEM] + [VMEM] * (3 + nk) + [ANY] * ne,
        out_specs=out_specs,
        scratch_shapes=scratch,
        compiler_params=pltpu.CompilerParams(vmem_limit_bytes=48 << 20),
        cost_estimate=pl.CostEstimate(
            flops=len(block_ids) << 31, bytes_accessed=8 << 20, transcendentals=len(block_ids) << 21
        ),
        name="last_away" if pack else "last_home",
    )(meta, order, q, *kvs, *state, *everything)


def join_kernel(acc, shift, came, out):
    for h in range(QH):
        total = acc[h, HD:HD + 1, :]
        here = shift[h] + jnp.log2(total)
        at = QH * HD + 8 * h
        level = came[at:at + 8, :].astype(F32)
        there = level[0:1] + level[1:2] + level[2:3]
        top = jnp.maximum(here, there)
        own, far = jnp.exp2(here - top), jnp.exp2(there - top)
        both = own + far
        mixed = acc[h, :HD, :] * (own / (total * both)) + came[h * HD:(h + 1) * HD, :].astype(F32) * (far / both)
        out[:, h * HD:(h + 1) * HD] = mixed.T.astype(BF16)


def join(state, came):
    return pl.pallas_call(
        join_kernel,
        out_shape=jax.ShapeDtypeStruct((TOK, QH * HD), BF16),
        in_specs=[VMEM] * 3,
        out_specs=VMEM,
        compiler_params=pltpu.CompilerParams(vmem_limit_bytes=32 << 20),
        name="join",
    )(*state, came)


def body(q0, keys, values, order):
    index = lax.axis_index("ctx")
    core = lax.axis_index("head") & 1
    y, z = index >> 2, index & 3
    even, odd = y ^ 1, (((y + 3) & 3 ^ 1) + 1) & 3
    key_y = jnp.where(core == 0, even, odd)
    query_y = jnp.where(core == 0, odd, even)
    meta = jnp.stack([index, key_y * 4 + z, query_y * 4 + z]).astype(jnp.int32)

    kv = jnp.concatenate([keys, values], axis=1)
    key_perm, query_perm = mate_perm(key_mate), mate_perm(query_mate)
    l_prev, l_next = send(kv, ring_perm(1)), send(kv, ring_perm(-1))
    p_own = send(kv, key_perm)
    q1 = send(q0, query_perm)
    half = TOK // 2
    l_far_a = send(l_prev[:half], ring_perm(1))
    l_far_b = send(l_next[half:], ring_perm(-1))
    p_prev, p_next = send(l_prev, key_perm), send(l_next, key_perm)
    p_far_a, p_far_b = send(l_far_a, key_perm), send(l_far_b, key_perm)

    state0 = diagonal(q0, kv)
    state1, state0 = stage(meta, order, [q1, q0], [2, 0], [kv, p_own], [(0, 0), (1, 0)], [None, state0], fresh=0)
    state1, state0 = stage(meta, order, [q1, q0], [2, 0], [l_prev, l_next], [(0, 3), (0, 1)], [state1, state0])
    (state1,) = stage(
        meta, order, [q1], [2], [p_prev, p_next, l_far_a, l_far_b], [(1, 3), (1, 1), (0, 2)], [state1]
    )
    everything = [kv, l_prev, l_next, l_far_a, l_far_b, p_own, p_prev, p_next, p_far_a, p_far_b]
    away = last_stage(meta, order, q1, 2, [p_far_a, p_far_b], [(1, 2)], state1, everything, True)
    came = send(away, query_perm)
    state0 = last_stage(
        meta, order, q0, 0, [p_prev, p_next, l_far_a, l_far_b, p_far_a, p_far_b],
        [(1, 3), (1, 1), (0, 2), (1, 2)], state0, everything, False,
    )
    return join(state0, came)


def solution(mesh):
    in_specs = (P("ctx", "head"), P("ctx", "head"), P("ctx", "head"), P())
    return jax.shard_map(body, mesh=mesh, in_specs=in_specs, out_specs=P("ctx", "head"), check_vma=False)
```

```python
import jax
import jax.numpy as jnp
from jax import lax
from jax.experimental import pallas as pl
from jax.experimental.pallas import tpu as pltpu
from jax.sharding import PartitionSpec as P

HD = 128
QH = 2
TOK = 1024
ROWS = HD + 8
SCALE = 168.0 ** (-0.5) * 1.4426950408889634
VMEM = pl.BlockSpec(memory_space=pltpu.VMEM)
SMEM = pl.BlockSpec(memory_space=pltpu.SMEM)
ANY = pl.BlockSpec(memory_space=pl.ANY)
F32 = jnp.float32
BF16 = jnp.bfloat16


def dot_last(a, b):
    return lax.dot_general(a, b, (((1,), (1,)), ((), ())), preferred_element_type=F32)


def dot_mid(a, b):
    return lax.dot_general(a, b, (((1,), (0,)), ((), ())), preferred_element_type=F32)


def key_mate(y, core):
    return y ^ 1 if core == 0 else (((y - 1) % 4 ^ 1) + 1) % 4


def query_mate(y, core):
    return key_mate(y, 1 - core)


def mate_perm(mate):
    return [
        ((y * 4 + z) * 16 + h, (mate(y, h % 2) * 4 + z) * 16 + h)
        for y in range(4) for z in range(4) for h in range(16)
    ]


def ring_perm(sign):
    return [
        ((y * 4 + z) * 16 + h, (y * 4 + (z + (sign if h % 2 == 0 else -sign)) % 4) * 16 + h)
        for y in range(4) for z in range(4) for h in range(16)
    ]


def send(array, perm):
    return lax.ppermute(array, ("ctx", "head"), perm)


def head(ref, h):
    return ref[:, h * HD:(h + 1) * HD]


def absorb(kb, vt, q_ref, acc, shift):
    scores = [dot_last(kb[...], head(q_ref, 0)), None]
    for h in range(QH):
        if h + 1 < QH:
            scores[h + 1] = dot_last(kb[...], head(q_ref, h + 1))
        weights = jnp.exp2(scores[h] * SCALE - shift[h]).astype(BF16)
        acc[h] += dot_mid(vt[...], weights)


OWN, NEAR_A, NEAR_B, FAR = range(4)


def rank_of(meta, order, base, kind):
    index = meta[base]
    offset = (0, meta[3], 4 - meta[3], 2)[kind]
    return order[(index & 12) | ((index + offset) & 3)]


def diagonal_kernel(q_ref, kv_ref, acc, shift, vt):
    vt[HD:, :] = jnp.ones((8, TOK), BF16)
    vt[:HD, :] = kv_ref[:, HD:].T
    keys = lax.broadcasted_iota(jnp.int32, (TOK, TOK), 0)
    rows = lax.broadcasted_iota(jnp.int32, (TOK, TOK), 1)
    for h in range(QH):
        scores = dot_last(kv_ref[:, :HD], head(q_ref, h)) * SCALE
        scores = jnp.where(keys <= rows, scores, -jnp.inf)
        shift[h] = jnp.max(scores, axis=0, keepdims=True)
        weights = jnp.exp2(scores - shift[h]).astype(BF16)
        acc[h] = dot_mid(vt[...], weights)


def diagonal(q, kv):
    return pl.pallas_call(
        diagonal_kernel,
        out_shape=[
            jax.ShapeDtypeStruct((QH, ROWS, TOK), F32),
            jax.ShapeDtypeStruct((QH, 1, TOK), F32),
        ],
        in_specs=[VMEM, VMEM],
        out_specs=[VMEM, VMEM],
        scratch_shapes=[pltpu.VMEM((ROWS, TOK), BF16)],
        compiler_params=pltpu.CompilerParams(vmem_limit_bytes=32 << 20),
        cost_estimate=pl.CostEstimate(flops=3 << 30, bytes_accessed=4 << 20, transcendentals=2 << 20),
        name="diagonal",
    )(q, kv)


ACC = (QH, ROWS, TOK)
SHIFT = (QH, 1, TOK)
SCRATCH = [pltpu.VMEM((TOK, HD), BF16), pltpu.VMEM((ROWS, TOK), BF16), pltpu.SMEM((16,), jnp.int32)]


def run_units(meta, order, q_refs, q_ids, kv_refs, blocks, accs, shifts, kb, vt, flags):
    nq, nb = len(q_ids), len(blocks)
    vt[HD:, :] = jnp.ones((8, TOK), BF16)
    for n, block in enumerate(blocks):
        rank = rank_of(meta, order, *block)
        for q, q_id in enumerate(q_ids):
            flags[n * nq + q] = (rank < order[meta[q_id]]).astype(jnp.int32)

    def one(n):
        some = flags[n * nq]
        for q in range(1, nq):
            some += flags[n * nq + q]

        @pl.when(some > 0)
        def _():
            for place in range(nb):
                @pl.when(n == place)
                def _():
                    kb[...] = kv_refs[place][:, :HD]
                    vt[:HD, :] = kv_refs[place][:, HD:].T

            def query(q):
                @pl.when(flags[n * nq + q] > 0)
                def _():
                    absorb(kb, vt, q_refs.at[q], accs.at[q], shifts.at[q])

            if nq == 1:
                query(0)
            else:
                pl.loop(0, nq)(query)

    if nb == 1:
        one(0)
    else:
        pl.loop(0, nb)(one)


def stage(meta, order, qs, kvs, blocks, states):
    nk = len(kvs)
    first = states[0] is None
    old = list(states[1]) if first else list(states)

    def kernel(*refs):
        meta_ref, order_ref = refs[:2]
        q_refs = refs[2:4]
        kv_refs = refs[4:4 + nk]
        old_acc, old_shift, acc, shift, q_both, kb, vt, flags = refs[4 + nk:]
        for q in range(2):
            q_both[q] = q_refs[q][...]
        if first:
            acc[1] = old_acc[...]
            shift[1] = old_shift[...]
            acc[0] = jnp.zeros(ACC, F32)
            for h in range(QH):
                sample = dot_last(kv_refs[0][:HD, :HD], head(q_refs[0], h))
                shift[0, h] = jnp.max(sample, axis=0, keepdims=True) * SCALE
        else:
            acc[...] = old_acc[...]
            shift[...] = old_shift[...]
        run_units(meta_ref, order_ref, q_both, [2, 0], kv_refs, blocks, acc, shift, kb, vt, flags)

    return pl.pallas_call(
        kernel,
        out_shape=[jax.ShapeDtypeStruct((2,) + ACC, F32), jax.ShapeDtypeStruct((2,) + SHIFT, F32)],
        in_specs=[SMEM, SMEM] + [VMEM] * (4 + nk),
        out_specs=[VMEM, VMEM],
        scratch_shapes=[pltpu.VMEM((2, TOK, QH * HD), BF16)] + SCRATCH,
        compiler_params=pltpu.CompilerParams(vmem_limit_bytes=32 << 20),
        cost_estimate=pl.CostEstimate(
            flops=2 * len(blocks) << 31, bytes_accessed=8 << 20, transcendentals=2 * len(blocks) << 21
        ),
        name="stage",
    )(meta, order, *qs, *kvs, *old)


def recompute(meta, order, q_id, q_ref, sources, acc, shift, buf, kb, vt):
    query_rank = order[meta[q_id]]
    acc[0] = jnp.zeros(ACC, F32)
    shift[0] = jnp.full(SHIFT, -1e30, F32)

    for n, source in enumerate(sources):
        rank = rank_of(meta, order, n // 4, n % 4)

        @pl.when(rank <= query_rank)
        def _():
            pltpu.sync_copy(source, buf)
            kb[...] = buf[:, :HD]
            vt[:HD, :] = buf[:, HD:].T

            @pl.loop(0, 16)
            def _(tile):
                h, start = tile & 1, pl.multiple_of((tile >> 1) * HD, HD)
                cols = pl.ds(start, HD)
                keys = lax.broadcasted_iota(jnp.int32, (TOK, HD), 0) + rank * TOK
                rows = lax.broadcasted_iota(jnp.int32, (TOK, HD), 1) + query_rank * TOK + start
                query = q_ref[cols, pl.ds(pl.multiple_of(h * HD, HD), HD)]
                scores = dot_last(kb[...], query) * SCALE
                scores = jnp.where(keys <= rows, scores, -jnp.inf)
                old = shift[0, h, :, cols]
                new = jnp.maximum(old, jnp.max(scores, axis=0, keepdims=True))
                weights = jnp.exp2(scores - new).astype(BF16)
                acc[0, h, :, cols] = acc[0, h, :, cols] * jnp.exp2(old - new) + dot_mid(vt[...], weights)
                shift[0, h, :, cols] = new


def closing(meta, order, q, q_id, kvs, blocks, state, everything, pack):
    nk, ne = len(kvs), len(everything)
    place = 0 if q_id == 2 else 1

    def kernel(*refs):
        meta_ref, order_ref, q_ref = refs[:3]
        kv_refs = refs[3:3 + nk]
        old_acc, old_shift = refs[3 + nk:5 + nk]
        all_refs = refs[5 + nk:5 + nk + ne]
        rest = refs[5 + nk + ne:]
        if pack:
            sent, acc, shift, buf, q_one, kb, vt, flags = rest
        else:
            acc, shift, buf, q_one, kb, vt, flags = rest
        at = place if old_acc.shape[0] == 2 else 0
        acc[0] = old_acc[at]
        shift[0] = old_shift[at]
        q_one[0] = q_ref[...]
        run_units(meta_ref, order_ref, q_one, [q_id], kv_refs, blocks, acc, shift, kb, vt, flags)
        if not ne:
            return
        query_rank = order_ref[meta_ref[q_id]]
        active = jnp.int32(0)
        for n in range(8):
            active += (rank_of(meta_ref, order_ref, n // 4, n % 4) <= query_rank).astype(jnp.int32)
        totals = jnp.concatenate([acc[0, h, HD:HD + 1, :] for h in range(QH)], axis=0)
        fine = jnp.logical_and(totals > 2.0 ** -60, totals < 2.0 ** 100)
        faults = jnp.sum(jnp.where(fine, 0.0, 1.0))

        @pl.when(jnp.logical_and(active > 0, faults > 0.0))
        def _():
            recompute(meta_ref, order_ref, q_id, q_ref, all_refs, acc, shift, buf, kb, vt)

        if pack:
            for h in range(QH):
                total = acc[0, h, HD:HD + 1, :]
                empty = total <= 0.0
                safe = jnp.where(empty, 1.0, total)
                sent[h * HD:(h + 1) * HD, :] = (acc[0, h, :HD, :] * (1.0 / safe)).astype(BF16)
                level = jnp.where(empty, -1e30, shift[0, h] + jnp.log2(safe))
                first = level.astype(BF16).astype(F32)
                second = (level - first).astype(BF16).astype(F32)
                third = level - first - second
                row = lax.broadcasted_iota(jnp.int32, (8, TOK), 0)
                packed = jnp.where(row == 0, first, jnp.where(row == 1, second, third))
                sent[QH * HD + 8 * h:QH * HD + 8 * h + 8, :] = packed.astype(BF16)

    state_shapes = [((1,) + ACC, F32), ((1,) + SHIFT, F32)]
    scratch = [pltpu.VMEM((TOK, 2 * HD), BF16), pltpu.VMEM((1, TOK, QH * HD), BF16)] + SCRATCH
    if pack:
        out_shape = jax.ShapeDtypeStruct((QH * HD + 16, TOK), BF16)
        out_specs = VMEM
        scratch = [pltpu.VMEM(*s) for s in state_shapes] + scratch
    else:
        out_shape = [jax.ShapeDtypeStruct(*s) for s in state_shapes]
        out_specs = [VMEM, VMEM]
    return pl.pallas_call(
        kernel,
        out_shape=out_shape,
        in_specs=[SMEM, SMEM] + [VMEM] * (3 + nk) + [ANY] * ne,
        out_specs=out_specs,
        scratch_shapes=scratch,
        compiler_params=pltpu.CompilerParams(vmem_limit_bytes=32 << 20),
        cost_estimate=pl.CostEstimate(
            flops=len(blocks) << 31, bytes_accessed=8 << 20, transcendentals=len(blocks) << 21
        ),
        name="away" if pack else "home" if ne else "guest",
    )(meta, order, q, *kvs, *state, *everything)


def join_kernel(acc, shift, came, out):
    for h in range(QH):
        total = acc[0, h, HD:HD + 1, :]
        here = shift[0, h] + jnp.log2(total)
        at = QH * HD + 8 * h
        level = came[at:at + 8, :].astype(F32)
        there = level[0:1] + level[1:2] + level[2:3]
        top = jnp.maximum(here, there)
        own, far = jnp.exp2(here - top), jnp.exp2(there - top)
        both = own + far
        mixed = acc[0, h, :HD, :] * (own / (total * both)) + came[h * HD:(h + 1) * HD, :].astype(F32) * (far / both)
        out[:, h * HD:(h + 1) * HD] = mixed.T.astype(BF16)


def join(state, came):
    return pl.pallas_call(
        join_kernel,
        out_shape=jax.ShapeDtypeStruct((TOK, QH * HD), BF16),
        in_specs=[VMEM] * 3,
        out_specs=VMEM,
        compiler_params=pltpu.CompilerParams(vmem_limit_bytes=32 << 20),
        name="join",
    )(*state, came)


def after(array, *others):
    return lax.optimization_barrier((array,) + others)[0]


def body(q0, keys, values, order):
    index = lax.axis_index("ctx")
    core = lax.axis_index("head") & 1
    y, z = index >> 2, index & 3
    even, odd = y ^ 1, (((y + 3) & 3 ^ 1) + 1) & 3
    key_y = jnp.where(core == 0, even, odd)
    query_y = jnp.where(core == 0, odd, even)
    meta = jnp.stack([index, key_y * 4 + z, query_y * 4 + z, jnp.where(core == 0, 3, 1)]).astype(jnp.int32)

    key_perm, query_perm = mate_perm(key_mate), mate_perm(query_mate)
    forth, back = ring_perm(1), ring_perm(-1)
    kv = jnp.concatenate([keys, values], axis=1)
    near_a = send(kv, forth)
    mate_own = send(kv, key_perm)
    q1 = send(q0, query_perm)
    state0 = diagonal(q0, kv)

    near_b = send(after(kv, near_a), back)
    mate_a = send(near_a, key_perm)
    qs = [after(q1, near_a), q0]
    state = stage(meta, order, qs, [kv, mate_own], [(0, OWN), (1, OWN)], [None, state0])

    far = send(after(near_a, near_b), forth)
    near_b = after(near_b, state[1])
    mate_b = send(near_b, key_perm)
    state = stage(
        meta, order, qs, [near_a, after(mate_a, near_b)], [(0, NEAR_A), (1, NEAR_A)], state
    )

    far = after(far, state[1])
    mate_far = send(far, key_perm)
    guest = closing(
        meta, order, q1, 2, [near_b, after(mate_b, far), far], [(0, NEAR_B), (1, NEAR_B), (0, FAR)], state, [], False
    )
    everything = [kv, near_a, near_b, far, mate_own, mate_a, mate_b, mate_far]
    away = closing(meta, order, q1, 2, [mate_far], [(1, FAR)], guest, everything, True)
    came = send(away, query_perm)
    own = closing(
        meta, order, q0, 0, [near_b, mate_b, far, mate_far],
        [(0, NEAR_B), (1, NEAR_B), (0, FAR), (1, FAR)], state, everything, False,
    )
    return join(own, came)


def solution(mesh):
    in_specs = (P("ctx", "head"), P("ctx", "head"), P("ctx", "head"), P())
    return jax.shard_map(body, mesh=mesh, in_specs=in_specs, out_specs=P("ctx", "head"), check_vma=False)
```

```python
import jax
import jax.numpy as jnp
from jax import lax
from jax.experimental import pallas as pl
from jax.experimental.pallas import tpu as pltpu
from jax.sharding import PartitionSpec as P

HD = 128
QH = 2
TOK = 1024
ROWS = HD + 8
SCALE = 168.0 ** (-0.5) * 1.4426950408889634
VMEM = pl.BlockSpec(memory_space=pltpu.VMEM)
SMEM = pl.BlockSpec(memory_space=pltpu.SMEM)
ANY = pl.BlockSpec(memory_space=pl.ANY)
F32 = jnp.float32
BF16 = jnp.bfloat16


def dot_last(a, b):
    return lax.dot_general(a, b, (((1,), (1,)), ((), ())), preferred_element_type=F32)


def dot_mid(a, b):
    return lax.dot_general(a, b, (((1,), (0,)), ((), ())), preferred_element_type=F32)


def key_mate(y, core):
    return y ^ 1 if core == 0 else (((y - 1) % 4 ^ 1) + 1) % 4


def query_mate(y, core):
    return key_mate(y, 1 - core)


def mate_perm(mate):
    return [
        ((y * 4 + z) * 16 + h, (mate(y, h % 2) * 4 + z) * 16 + h)
        for y in range(4) for z in range(4) for h in range(16)
    ]


def ring_perm(sign):
    return [
        ((y * 4 + z) * 16 + h, (y * 4 + (z + (sign if h % 2 == 0 else -sign)) % 4) * 16 + h)
        for y in range(4) for z in range(4) for h in range(16)
    ]


def send(array, perm):
    return lax.ppermute(array, ("ctx", "head"), perm)


def head(ref, h):
    return ref[:, h * HD:(h + 1) * HD]


def absorb(kb, vt, q_ref, acc, shift):
    scores = [dot_last(kb[...], head(q_ref, 0)), None]
    for h in range(QH):
        if h + 1 < QH:
            scores[h + 1] = dot_last(kb[...], head(q_ref, h + 1))
        weights = jnp.exp2(scores[h] * SCALE - shift[h]).astype(BF16)
        acc[h] += dot_mid(vt[...], weights)


OWN, NEAR_A, NEAR_B, FAR = range(4)


def rank_of(meta, order, base, kind):
    index = meta[base]
    offset = (0, meta[3], 4 - meta[3], 2)[kind]
    return order[(index & 12) | ((index + offset) & 3)]


def diagonal_kernel(q_ref, kv_ref, acc, shift, vt):
    vt[HD:, :] = jnp.ones((8, TOK), BF16)
    vt[:HD, :] = kv_ref[:, HD:].T
    keys = lax.broadcasted_iota(jnp.int32, (TOK, TOK), 0)
    rows = lax.broadcasted_iota(jnp.int32, (TOK, TOK), 1)
    for h in range(QH):
        scores = dot_last(kv_ref[:, :HD], head(q_ref, h)) * SCALE
        scores = jnp.where(keys <= rows, scores, -jnp.inf)
        shift[h] = jnp.max(scores, axis=0, keepdims=True)
        weights = jnp.exp2(scores - shift[h]).astype(BF16)
        acc[h] = dot_mid(vt[...], weights)


def diagonal(q, kv):
    return pl.pallas_call(
        diagonal_kernel,
        out_shape=[
            jax.ShapeDtypeStruct((QH, ROWS, TOK), F32),
            jax.ShapeDtypeStruct((QH, 1, TOK), F32),
        ],
        in_specs=[VMEM, VMEM],
        out_specs=[VMEM, VMEM],
        scratch_shapes=[pltpu.VMEM((ROWS, TOK), BF16)],
        compiler_params=pltpu.CompilerParams(vmem_limit_bytes=32 << 20),
        cost_estimate=pl.CostEstimate(flops=3 << 30, bytes_accessed=4 << 20, transcendentals=2 << 20),
        name="diagonal",
    )(q, kv)


ACC = (QH, ROWS, TOK)
SHIFT = (QH, 1, TOK)
SCRATCH = [pltpu.VMEM((TOK, HD), BF16), pltpu.VMEM((ROWS, TOK), BF16), pltpu.SMEM((16,), jnp.int32)]


def run_units(meta, order, q_refs, q_ids, kv_refs, blocks, accs, shifts, kb, vt, flags):
    nq, nb = len(q_ids), len(blocks)
    vt[HD:, :] = jnp.ones((8, TOK), BF16)
    for n, block in enumerate(blocks):
        rank = rank_of(meta, order, *block)
        for q, q_id in enumerate(q_ids):
            flags[n * nq + q] = (rank < order[meta[q_id]]).astype(jnp.int32)

    def one(n):
        some = flags[n * nq]
        for q in range(1, nq):
            some += flags[n * nq + q]

        @pl.when(some > 0)
        def _():
            for place in range(nb):
                @pl.when(n == place)
                def _():
                    kb[...] = kv_refs[place][:, :HD]
                    vt[:HD, :] = kv_refs[place][:, HD:].T

            def query(q):
                @pl.when(flags[n * nq + q] > 0)
                def _():
                    absorb(kb, vt, q_refs.at[q], accs.at[q], shifts.at[q])

            if nq == 1:
                query(0)
            else:
                pl.loop(0, nq)(query)

    if nb == 1:
        one(0)
    else:
        pl.loop(0, nb)(one)


def stage(meta, order, qs, kvs, blocks, states):
    nk = len(kvs)
    first = states[0] is None
    old = list(states[1]) if first else list(states)

    def kernel(*refs):
        meta_ref, order_ref = refs[:2]
        q_refs = refs[2:4]
        kv_refs = refs[4:4 + nk]
        old_acc, old_shift, acc, shift, q_both, kb, vt, flags = refs[4 + nk:]
        for q in range(2):
            q_both[q] = q_refs[q][...]
        if first:
            acc[1] = old_acc[...]
            shift[1] = old_shift[...]
            acc[0] = jnp.zeros(ACC, F32)
            for h in range(QH):
                sample = dot_last(kv_refs[0][:HD, :HD], head(q_refs[0], h))
                shift[0, h] = jnp.max(sample, axis=0, keepdims=True) * SCALE
        else:
            acc[...] = old_acc[...]
            shift[...] = old_shift[...]
        run_units(meta_ref, order_ref, q_both, [2, 0], kv_refs, blocks, acc, shift, kb, vt, flags)

    return pl.pallas_call(
        kernel,
        out_shape=[jax.ShapeDtypeStruct((2,) + ACC, F32), jax.ShapeDtypeStruct((2,) + SHIFT, F32)],
        in_specs=[SMEM, SMEM] + [VMEM] * (4 + nk),
        out_specs=[VMEM, VMEM],
        scratch_shapes=[pltpu.VMEM((2, TOK, QH * HD), BF16)] + SCRATCH,
        compiler_params=pltpu.CompilerParams(vmem_limit_bytes=32 << 20),
        cost_estimate=pl.CostEstimate(
            flops=2 * len(blocks) << 31, bytes_accessed=8 << 20, transcendentals=2 * len(blocks) << 21
        ),
        name="stage",
    )(meta, order, *qs, *kvs, *old)


def recompute(meta, order, q_id, q_ref, sources, acc, shift, buf, kb, vt):
    query_rank = order[meta[q_id]]
    acc[0] = jnp.zeros(ACC, F32)
    shift[0] = jnp.full(SHIFT, -1e30, F32)

    for n, source in enumerate(sources):
        rank = rank_of(meta, order, n // 4, n % 4)

        @pl.when(rank <= query_rank)
        def _():
            pltpu.sync_copy(source, buf)
            kb[...] = buf[:, :HD]
            vt[:HD, :] = buf[:, HD:].T

            @pl.loop(0, 16)
            def _(tile):
                h, start = tile & 1, pl.multiple_of((tile >> 1) * HD, HD)
                cols = pl.ds(start, HD)
                keys = lax.broadcasted_iota(jnp.int32, (TOK, HD), 0) + rank * TOK
                rows = lax.broadcasted_iota(jnp.int32, (TOK, HD), 1) + query_rank * TOK + start
                query = q_ref[cols, pl.ds(pl.multiple_of(h * HD, HD), HD)]
                scores = dot_last(kb[...], query) * SCALE
                scores = jnp.where(keys <= rows, scores, -jnp.inf)
                old = shift[0, h, :, cols]
                new = jnp.maximum(old, jnp.max(scores, axis=0, keepdims=True))
                weights = jnp.exp2(scores - new).astype(BF16)
                acc[0, h, :, cols] = acc[0, h, :, cols] * jnp.exp2(old - new) + dot_mid(vt[...], weights)
                shift[0, h, :, cols] = new


def closing(meta, order, q, q_id, kvs, blocks, state, everything, pack):
    nk, ne = len(kvs), len(everything)
    place = 0 if q_id == 2 else 1

    def kernel(*refs):
        meta_ref, order_ref, q_ref = refs[:3]
        kv_refs = refs[3:3 + nk]
        old_acc, old_shift = refs[3 + nk:5 + nk]
        all_refs = refs[5 + nk:5 + nk + ne]
        rest = refs[5 + nk + ne:]
        if pack:
            sent, acc, shift, buf, q_one, kb, vt, flags = rest
        else:
            acc, shift, buf, q_one, kb, vt, flags = rest
        at = place if old_acc.shape[0] == 2 else 0
        acc[0] = old_acc[at]
        shift[0] = old_shift[at]
        q_one[0] = q_ref[...]
        run_units(meta_ref, order_ref, q_one, [q_id], kv_refs, blocks, acc, shift, kb, vt, flags)
        if not ne:
            return
        query_rank = order_ref[meta_ref[q_id]]
        active = jnp.int32(0)
        for n in range(8):
            active += (rank_of(meta_ref, order_ref, n // 4, n % 4) <= query_rank).astype(jnp.int32)
        totals = jnp.concatenate([acc[0, h, HD:HD + 1, :] for h in range(QH)], axis=0)
        fine = jnp.logical_and(totals > 2.0 ** -60, totals < 2.0 ** 100)
        faults = jnp.sum(jnp.where(fine, 0.0, 1.0))

        @pl.when(jnp.logical_and(active > 0, faults > 0.0))
        def _():
            recompute(meta_ref, order_ref, q_id, q_ref, all_refs, acc, shift, buf, kb, vt)

        if pack:
            for h in range(QH):
                total = acc[0, h, HD:HD + 1, :]
                empty = total <= 0.0
                safe = jnp.where(empty, 1.0, total)
                sent[h * HD:(h + 1) * HD, :] = (acc[0, h, :HD, :] * (1.0 / safe)).astype(BF16)
                level = jnp.where(empty, -1e30, shift[0, h] + jnp.log2(safe))
                first = level.astype(BF16).astype(F32)
                second = (level - first).astype(BF16).astype(F32)
                third = level - first - second
                row = lax.broadcasted_iota(jnp.int32, (8, TOK), 0)
                packed = jnp.where(row == 0, first, jnp.where(row == 1, second, third))
                sent[QH * HD + 8 * h:QH * HD + 8 * h + 8, :] = packed.astype(BF16)

    state_shapes = [((1,) + ACC, F32), ((1,) + SHIFT, F32)]
    scratch = [pltpu.VMEM((TOK, 2 * HD), BF16), pltpu.VMEM((1, TOK, QH * HD), BF16)] + SCRATCH
    if pack:
        out_shape = jax.ShapeDtypeStruct((QH * HD + 16, TOK), BF16)
        out_specs = VMEM
        scratch = [pltpu.VMEM(*s) for s in state_shapes] + scratch
    else:
        out_shape = [jax.ShapeDtypeStruct(*s) for s in state_shapes]
        out_specs = [VMEM, VMEM]
    return pl.pallas_call(
        kernel,
        out_shape=out_shape,
        in_specs=[SMEM, SMEM] + [VMEM] * (3 + nk) + [ANY] * ne,
        out_specs=out_specs,
        scratch_shapes=scratch,
        compiler_params=pltpu.CompilerParams(vmem_limit_bytes=32 << 20),
        cost_estimate=pl.CostEstimate(
            flops=len(blocks) << 31, bytes_accessed=8 << 20, transcendentals=len(blocks) << 21
        ),
        name="away" if pack else "home" if ne else "guest",
    )(meta, order, q, *kvs, *state, *everything)


def join_kernel(acc, shift, came, out):
    for h in range(QH):
        total = acc[0, h, HD:HD + 1, :]
        here = shift[0, h] + jnp.log2(total)
        at = QH * HD + 8 * h
        level = came[at:at + 8, :].astype(F32)
        there = level[0:1] + level[1:2] + level[2:3]
        top = jnp.maximum(here, there)
        own, far = jnp.exp2(here - top), jnp.exp2(there - top)
        both = own + far
        mixed = acc[0, h, :HD, :] * (own / (total * both)) + came[h * HD:(h + 1) * HD, :].astype(F32) * (far / both)
        out[:, h * HD:(h + 1) * HD] = mixed.T.astype(BF16)


def join(state, came):
    return pl.pallas_call(
        join_kernel,
        out_shape=jax.ShapeDtypeStruct((TOK, QH * HD), BF16),
        in_specs=[VMEM] * 3,
        out_specs=VMEM,
        compiler_params=pltpu.CompilerParams(vmem_limit_bytes=32 << 20),
        name="join",
    )(*state, came)


def after(array, *others):
    return lax.optimization_barrier((array,) + others)[0]


def pack_kernel(keys, values, kv):
    kv[:, :HD] = keys[...]
    kv[:, HD:] = values[...]


def packed_kv(keys, values):
    return pl.pallas_call(
        pack_kernel,
        out_shape=jax.ShapeDtypeStruct((TOK, 2 * HD), BF16),
        in_specs=[VMEM] * 2,
        out_specs=VMEM,
        name="pack_kv",
    )(keys, values)


def body(q0, keys, values, order):
    index = lax.axis_index("ctx")
    core = lax.axis_index("head") & 1
    y, z = index >> 2, index & 3
    even, odd = y ^ 1, (((y + 3) & 3 ^ 1) + 1) & 3
    key_y = jnp.where(core == 0, even, odd)
    query_y = jnp.where(core == 0, odd, even)
    meta = jnp.stack([index, key_y * 4 + z, query_y * 4 + z, jnp.where(core == 0, 3, 1)]).astype(jnp.int32)

    key_perm, query_perm = mate_perm(key_mate), mate_perm(query_mate)
    forth, back = ring_perm(1), ring_perm(-1)
    kv = packed_kv(keys, values)
    near_a = send(kv, forth)
    near_b = send(kv, back)
    mate_own = send(kv, key_perm)
    q1 = send(q0, query_perm)
    state0 = diagonal(q0, kv)
    qs = [q1, q0]
    state = stage(meta, order, qs, [kv, mate_own], [(0, OWN), (1, OWN)], [None, state0])

    near_a, near_b = after((near_a, near_b), state[1])
    far = send(near_a, forth)
    mate_a = send(near_a, key_perm)
    mate_b = send(near_b, key_perm)
    state = stage(meta, order, [q1, after(q0, near_a, near_b)], [near_a, near_b], [(0, NEAR_A), (0, NEAR_B)], state)

    far, mate_a, mate_b = after((far, mate_a, mate_b), state[1])
    mate_far = send(far, key_perm)
    guest = closing(
        meta, order, q1, 2, [after(mate_a, far), mate_b, far], [(1, NEAR_A), (1, NEAR_B), (0, FAR)], state, [], False
    )
    everything = [kv, near_a, near_b, far, mate_own, mate_a, mate_b, mate_far]
    away = closing(meta, order, q1, 2, [mate_far], [(1, FAR)], guest, everything, True)
    came = send(away, query_perm)
    own = closing(
        meta, order, q0, 0, [mate_a, mate_b, far, mate_far],
        [(1, NEAR_A), (1, NEAR_B), (0, FAR), (1, FAR)], state, everything, False,
    )
    return join(own, came)


def solution(mesh):
    in_specs = (P("ctx", "head"), P("ctx", "head"), P("ctx", "head"), P())
    return jax.shard_map(body, mesh=mesh, in_specs=in_specs, out_specs=P("ctx", "head"), check_vma=False)
```

```python
import jax
import jax.numpy as jnp
from jax import lax
from jax.experimental import pallas as pl
from jax.experimental.pallas import tpu as pltpu
from jax.sharding import PartitionSpec as P

HD = 128
QH = 2
TOK = 1024
ROWS = HD + 8
SCALE = 168.0 ** (-0.5) * 1.4426950408889634
VMEM = pl.BlockSpec(memory_space=pltpu.VMEM)
SMEM = pl.BlockSpec(memory_space=pltpu.SMEM)
ANY = pl.BlockSpec(memory_space=pl.ANY)
F32 = jnp.float32
BF16 = jnp.bfloat16


def dot_last(a, b):
    return lax.dot_general(a, b, (((1,), (1,)), ((), ())), preferred_element_type=F32)


def dot_mid(a, b):
    return lax.dot_general(a, b, (((1,), (0,)), ((), ())), preferred_element_type=F32)


def key_mate(y, core):
    return y ^ 1 if core == 0 else (((y - 1) % 4 ^ 1) + 1) % 4


def query_mate(y, core):
    return key_mate(y, 1 - core)


def mate_perm(mate):
    return [
        ((y * 4 + z) * 16 + h, (mate(y, h % 2) * 4 + z) * 16 + h)
        for y in range(4) for z in range(4) for h in range(16)
    ]


def ring_perm(sign):
    return [
        ((y * 4 + z) * 16 + h, (y * 4 + (z + (sign if h % 2 == 0 else -sign)) % 4) * 16 + h)
        for y in range(4) for z in range(4) for h in range(16)
    ]


def send(array, perm):
    return lax.ppermute(array, ("ctx", "head"), perm)


def head(ref, h):
    return ref[:, h * HD:(h + 1) * HD]


def fill_values(vt, kv_ref):
    for n in range(TOK // HD):
        tile = slice(n * HD, (n + 1) * HD)
        vt[:HD, tile] = kv_ref[tile, HD:]


def absorb(kb, vt, q_ref, acc, shift):
    scores = [dot_last(kb[...], head(q_ref, 0)), None]
    for h in range(QH):
        if h + 1 < QH:
            scores[h + 1] = dot_last(kb[...], head(q_ref, h + 1))
        weights = jnp.exp2(scores[h] * SCALE - shift[h]).astype(BF16)
        acc[h] += dot_mid(vt[...], weights)


OWN, NEAR_A, NEAR_B, FAR = range(4)


def rank_of(meta, order, base, kind):
    index = meta[base]
    offset = (0, meta[3], 4 - meta[3], 2)[kind]
    return order[(index & 12) | ((index + offset) & 3)]


def diagonal_kernel(q_ref, kv_ref, acc, shift, vt):
    vt[HD:, :] = jnp.ones((8, TOK), BF16)
    fill_values(vt, kv_ref)
    keys = lax.broadcasted_iota(jnp.int32, (TOK, TOK), 0)
    rows = lax.broadcasted_iota(jnp.int32, (TOK, TOK), 1)
    for h in range(QH):
        scores = dot_last(kv_ref[:, :HD], head(q_ref, h)) * SCALE
        scores = jnp.where(keys <= rows, scores, -jnp.inf)
        shift[h] = jnp.max(scores, axis=0, keepdims=True)
        weights = jnp.exp2(scores - shift[h]).astype(BF16)
        acc[h] = dot_mid(vt[...], weights)


def diagonal(q, kv):
    return pl.pallas_call(
        diagonal_kernel,
        out_shape=[
            jax.ShapeDtypeStruct((QH, ROWS, TOK), F32),
            jax.ShapeDtypeStruct((QH, 1, TOK), F32),
        ],
        in_specs=[VMEM, VMEM],
        out_specs=[VMEM, VMEM],
        scratch_shapes=[pltpu.VMEM((ROWS, TOK), BF16)],
        compiler_params=pltpu.CompilerParams(vmem_limit_bytes=32 << 20),
        cost_estimate=pl.CostEstimate(flops=3 << 30, bytes_accessed=4 << 20, transcendentals=2 << 20),
        name="diagonal",
    )(q, kv)


ACC = (QH, ROWS, TOK)
SHIFT = (QH, 1, TOK)
SCRATCH = [pltpu.VMEM((TOK, HD), BF16), pltpu.VMEM((ROWS, TOK), BF16), pltpu.SMEM((16,), jnp.int32)]


def run_units(meta, order, q_refs, q_ids, kv_refs, blocks, accs, shifts, kb, vt, flags):
    nq, nb = len(q_ids), len(blocks)
    vt[HD:, :] = jnp.ones((8, TOK), BF16)
    for n, block in enumerate(blocks):
        rank = rank_of(meta, order, *block)
        for q, q_id in enumerate(q_ids):
            flags[n * nq + q] = (rank < order[meta[q_id]]).astype(jnp.int32)

    def one(n):
        some = flags[n * nq]
        for q in range(1, nq):
            some += flags[n * nq + q]

        @pl.when(some > 0)
        def _():
            for place in range(nb):
                @pl.when(n == place)
                def _():
                    kb[...] = kv_refs[place][:, :HD]
                    fill_values(vt, kv_refs[place])

            def query(q):
                @pl.when(flags[n * nq + q] > 0)
                def _():
                    absorb(kb, vt, q_refs.at[q], accs.at[q], shifts.at[q])

            if nq == 1:
                query(0)
            else:
                pl.loop(0, nq)(query)

    if nb == 1:
        one(0)
    else:
        pl.loop(0, nb)(one)


def stage(meta, order, qs, kvs, blocks, states):
    nk = len(kvs)
    first = states[0] is None
    old = list(states[1]) if first else list(states)

    def kernel(*refs):
        meta_ref, order_ref = refs[:2]
        q_refs = refs[2:4]
        kv_refs = refs[4:4 + nk]
        old_acc, old_shift, acc, shift, q_both, kb, vt, flags = refs[4 + nk:]
        for q in range(2):
            q_both[q] = q_refs[q][...]
        if first:
            acc[1] = old_acc[...]
            shift[1] = old_shift[...]
            acc[0] = jnp.zeros(ACC, F32)
            for h in range(QH):
                sample = dot_last(kv_refs[0][:HD, :HD], head(q_refs[0], h))
                shift[0, h] = jnp.max(sample, axis=0, keepdims=True) * SCALE
        else:
            acc[...] = old_acc[...]
            shift[...] = old_shift[...]
        run_units(meta_ref, order_ref, q_both, [2, 0], kv_refs, blocks, acc, shift, kb, vt, flags)

    return pl.pallas_call(
        kernel,
        out_shape=[jax.ShapeDtypeStruct((2,) + ACC, F32), jax.ShapeDtypeStruct((2,) + SHIFT, F32)],
        in_specs=[SMEM, SMEM] + [VMEM] * (4 + nk),
        out_specs=[VMEM, VMEM],
        scratch_shapes=[pltpu.VMEM((2, TOK, QH * HD), BF16)] + SCRATCH,
        compiler_params=pltpu.CompilerParams(vmem_limit_bytes=32 << 20),
        cost_estimate=pl.CostEstimate(
            flops=2 * len(blocks) << 31, bytes_accessed=8 << 20, transcendentals=2 * len(blocks) << 21
        ),
        name="stage",
    )(meta, order, *qs, *kvs, *old)


def recompute(meta, order, q_id, q_ref, sources, acc, shift, buf, kb, vt):
    query_rank = order[meta[q_id]]
    acc[0] = jnp.zeros(ACC, F32)
    shift[0] = jnp.full(SHIFT, -1e30, F32)

    for n, source in enumerate(sources):
        rank = rank_of(meta, order, n // 4, n % 4)

        @pl.when(rank <= query_rank)
        def _():
            pltpu.sync_copy(source, buf)
            kb[...] = buf[:, :HD]
            fill_values(vt, buf)

            @pl.loop(0, 16)
            def _(tile):
                h, start = tile & 1, pl.multiple_of((tile >> 1) * HD, HD)
                cols = pl.ds(start, HD)
                keys = lax.broadcasted_iota(jnp.int32, (TOK, HD), 0) + rank * TOK
                rows = lax.broadcasted_iota(jnp.int32, (TOK, HD), 1) + query_rank * TOK + start
                query = q_ref[cols, pl.ds(pl.multiple_of(h * HD, HD), HD)]
                scores = dot_last(kb[...], query) * SCALE
                scores = jnp.where(keys <= rows, scores, -jnp.inf)
                old = shift[0, h, :, cols]
                new = jnp.maximum(old, jnp.max(scores, axis=0, keepdims=True))
                weights = jnp.exp2(scores - new).astype(BF16)
                acc[0, h, :, cols] = acc[0, h, :, cols] * jnp.exp2(old - new) + dot_mid(vt[...], weights)
                shift[0, h, :, cols] = new


def closing(meta, order, q, q_id, kvs, blocks, state, everything, pack):
    nk, ne = len(kvs), len(everything)
    place = 0 if q_id == 2 else 1

    def kernel(*refs):
        meta_ref, order_ref, q_ref = refs[:3]
        kv_refs = refs[3:3 + nk]
        old_acc, old_shift = refs[3 + nk:5 + nk]
        all_refs = refs[5 + nk:5 + nk + ne]
        rest = refs[5 + nk + ne:]
        if pack:
            sent, acc, shift, buf, q_one, kb, vt, flags = rest
        else:
            acc, shift, buf, q_one, kb, vt, flags = rest
        at = place if old_acc.shape[0] == 2 else 0
        acc[0] = old_acc[at]
        shift[0] = old_shift[at]
        q_one[0] = q_ref[...]
        run_units(meta_ref, order_ref, q_one, [q_id], kv_refs, blocks, acc, shift, kb, vt, flags)
        if not ne:
            return
        query_rank = order_ref[meta_ref[q_id]]
        active = jnp.int32(0)
        for n in range(8):
            active += (rank_of(meta_ref, order_ref, n // 4, n % 4) <= query_rank).astype(jnp.int32)
        totals = jnp.concatenate([acc[0, h, HD:HD + 1, :] for h in range(QH)], axis=0)
        fine = jnp.logical_and(totals > 2.0 ** -60, totals < 2.0 ** 100)
        faults = jnp.sum(jnp.where(fine, 0.0, 1.0))

        @pl.when(jnp.logical_and(active > 0, faults > 0.0))
        def _():
            recompute(meta_ref, order_ref, q_id, q_ref, all_refs, acc, shift, buf, kb, vt)

        if pack:
            for h in range(QH):
                total = acc[0, h, HD:HD + 1, :]
                empty = total <= 0.0
                safe = jnp.where(empty, 1.0, total)
                sent[h * HD:(h + 1) * HD, :] = (acc[0, h, :HD, :] * (1.0 / safe)).astype(BF16)
                level = jnp.where(empty, -1e30, shift[0, h] + jnp.log2(safe))
                first = level.astype(BF16).astype(F32)
                second = (level - first).astype(BF16).astype(F32)
                third = level - first - second
                row = lax.broadcasted_iota(jnp.int32, (8, TOK), 0)
                packed = jnp.where(row == 0, first, jnp.where(row == 1, second, third))
                sent[QH * HD + 8 * h:QH * HD + 8 * h + 8, :] = packed.astype(BF16)

    state_shapes = [((1,) + ACC, F32), ((1,) + SHIFT, F32)]
    scratch = [pltpu.VMEM((TOK, 2 * HD), BF16), pltpu.VMEM((1, TOK, QH * HD), BF16)] + SCRATCH
    if pack:
        out_shape = jax.ShapeDtypeStruct((QH * HD + 16, TOK), BF16)
        out_specs = VMEM
        scratch = [pltpu.VMEM(*s) for s in state_shapes] + scratch
    else:
        out_shape = [jax.ShapeDtypeStruct(*s) for s in state_shapes]
        out_specs = [VMEM, VMEM]
    return pl.pallas_call(
        kernel,
        out_shape=out_shape,
        in_specs=[SMEM, SMEM] + [VMEM] * (3 + nk) + [ANY] * ne,
        out_specs=out_specs,
        scratch_shapes=scratch,
        compiler_params=pltpu.CompilerParams(vmem_limit_bytes=32 << 20),
        cost_estimate=pl.CostEstimate(
            flops=len(blocks) << 31, bytes_accessed=8 << 20, transcendentals=len(blocks) << 21
        ),
        name="away" if pack else "home" if ne else "guest",
    )(meta, order, q, *kvs, *state, *everything)


def join_kernel(acc, shift, came, out):
    for h in range(QH):
        total = acc[0, h, HD:HD + 1, :]
        here = shift[0, h] + jnp.log2(total)
        at = QH * HD + 8 * h
        level = came[at:at + 8, :].astype(F32)
        there = level[0:1] + level[1:2] + level[2:3]
        top = jnp.maximum(here, there)
        own, far = jnp.exp2(here - top), jnp.exp2(there - top)
        both = own + far
        mixed = acc[0, h, :HD, :] * (own / (total * both)) + came[h * HD:(h + 1) * HD, :].astype(F32) * (far / both)
        out[:, h * HD:(h + 1) * HD] = mixed.T.astype(BF16)


def join(state, came):
    return pl.pallas_call(
        join_kernel,
        out_shape=jax.ShapeDtypeStruct((TOK, QH * HD), BF16),
        in_specs=[VMEM] * 3,
        out_specs=VMEM,
        compiler_params=pltpu.CompilerParams(vmem_limit_bytes=32 << 20),
        name="join",
    )(*state, came)


def pack_kernel(keys, values, kv):
    kv[:, :HD] = keys[...]
    for n in range(TOK // HD):
        tile = slice(n * HD, (n + 1) * HD)
        kv[tile, HD:] = values[tile, :].T


def packed_kv(keys, values):
    return pl.pallas_call(
        pack_kernel,
        out_shape=jax.ShapeDtypeStruct((TOK, 2 * HD), BF16),
        in_specs=[VMEM] * 2,
        out_specs=VMEM,
        name="pack_kv",
    )(keys, values)


def body(q0, keys, values, order):
    index = lax.axis_index("ctx")
    core = lax.axis_index("head") & 1
    y, z = index >> 2, index & 3
    even, odd = y ^ 1, (((y + 3) & 3 ^ 1) + 1) & 3
    key_y = jnp.where(core == 0, even, odd)
    query_y = jnp.where(core == 0, odd, even)
    meta = jnp.stack([index, key_y * 4 + z, query_y * 4 + z, jnp.where(core == 0, 3, 1)]).astype(jnp.int32)

    key_perm, query_perm = mate_perm(key_mate), mate_perm(query_mate)
    forth, back = ring_perm(1), ring_perm(-1)
    kv = packed_kv(keys, values)
    near_a = send(kv, forth)
    near_b = send(kv, back)
    acc, shift = diagonal(q0, kv)
    mate_own = send(kv, key_perm)
    q1 = send(q0, query_perm)
    qs = [q1, q0]
    state = stage(meta, order, qs, [kv, mate_own], [(0, OWN), (1, OWN)], [None, (acc, shift)])

    near_a, near_b, shift = lax.optimization_barrier((near_a, near_b, state[1]))
    far = send(near_a, forth)
    mate_a = send(near_a, key_perm)
    mate_b = send(near_b, key_perm)
    state = stage(meta, order, qs, [near_a, near_b], [(0, NEAR_A), (0, NEAR_B)], [state[0], shift])

    far, shift = lax.optimization_barrier((far, state[1]))
    state = [state[0], shift]
    mate_far = send(far, key_perm)
    guest = closing(
        meta, order, q1, 2, [mate_a, mate_b, far], [(1, NEAR_A), (1, NEAR_B), (0, FAR)], state, [], False
    )
    everything = [kv, near_a, near_b, far, mate_own, mate_a, mate_b, mate_far]
    away = closing(meta, order, q1, 2, [mate_far], [(1, FAR)], guest, everything, True)
    came = send(away, query_perm)
    own = closing(
        meta, order, q0, 0, [mate_a, mate_b, far, mate_far],
        [(1, NEAR_A), (1, NEAR_B), (0, FAR), (1, FAR)], state, everything, False,
    )
    return join(own, came)


def solution(mesh):
    in_specs = (P("ctx", "head"), P("ctx", "head"), P("ctx", "head"), P())
    return jax.shard_map(body, mesh=mesh, in_specs=in_specs, out_specs=P("ctx", "head"), check_vma=False)
```

```python
import jax
import jax.numpy as jnp
from jax import lax
from jax.experimental import pallas as pl
from jax.experimental.pallas import tpu as pltpu
from jax.sharding import PartitionSpec as P

HD = 128
QH = 2
TOK = 1024
HALF = TOK // 2
ROWS = HD + 8
SCALE = 168.0 ** (-0.5) * 1.4426950408889634
VMEM = pl.BlockSpec(memory_space=pltpu.VMEM)
SMEM = pl.BlockSpec(memory_space=pltpu.SMEM)
ANY = pl.BlockSpec(memory_space=pl.ANY)
F32 = jnp.float32
BF16 = jnp.bfloat16


def dot_last(a, b):
    return lax.dot_general(a, b, (((1,), (1,)), ((), ())), preferred_element_type=F32)


def dot_mid(a, b):
    return lax.dot_general(a, b, (((1,), (0,)), ((), ())), preferred_element_type=F32)


def key_mate(y, core):
    return y ^ 1 if core == 0 else (((y - 1) % 4 ^ 1) + 1) % 4


def query_mate(y, core):
    return key_mate(y, 1 - core)


def mate_perm(mate):
    return [
        ((y * 4 + z) * 16 + h, (mate(y, h % 2) * 4 + z) * 16 + h)
        for y in range(4) for z in range(4) for h in range(16)
    ]


def ring_perm(sign):
    return [
        ((y * 4 + z) * 16 + h, (y * 4 + (z + (sign if h % 2 == 0 else -sign)) % 4) * 16 + h)
        for y in range(4) for z in range(4) for h in range(16)
    ]


def send(array, perm):
    return lax.ppermute(array, ("ctx", "head"), perm)


def head(ref, h):
    return ref[:, h * HD:(h + 1) * HD]


def fill_values(vt, kv_ref):
    for n in range(kv_ref.shape[0] // HD):
        tile = slice(n * HD, (n + 1) * HD)
        vt[:HD, tile] = kv_ref[tile, HD:]


def absorb(kb, vt, q_ref, acc, shift):
    scores = [dot_last(kb[...], head(q_ref, 0)), None]
    for h in range(QH):
        if h + 1 < QH:
            scores[h + 1] = dot_last(kb[...], head(q_ref, h + 1))
        weights = jnp.exp2(scores[h] * SCALE - shift[h]).astype(BF16)
        acc[h] += dot_mid(vt[...], weights)


OWN, NEAR_A, NEAR_B, FAR = range(4)


def rank_of(meta, order, base, kind):
    index = meta[base]
    offset = (0, meta[3], 4 - meta[3], 2)[kind]
    return order[(index & 12) | ((index + offset) & 3)]


def diagonal_kernel(q_ref, kv_ref, acc, shift, vt):
    vt[HD:, :] = jnp.ones((8, TOK), BF16)
    fill_values(vt, kv_ref)
    keys = lax.broadcasted_iota(jnp.int32, (TOK, TOK), 0)
    rows = lax.broadcasted_iota(jnp.int32, (TOK, TOK), 1)
    for h in range(QH):
        scores = dot_last(kv_ref[:, :HD], head(q_ref, h)) * SCALE
        scores = jnp.where(keys <= rows, scores, -jnp.inf)
        shift[h] = jnp.max(scores, axis=0, keepdims=True)
        weights = jnp.exp2(scores - shift[h]).astype(BF16)
        acc[h] = dot_mid(vt[...], weights)


def diagonal(q, kv):
    return pl.pallas_call(
        diagonal_kernel,
        out_shape=[
            jax.ShapeDtypeStruct((QH, ROWS, TOK), F32),
            jax.ShapeDtypeStruct((QH, 1, TOK), F32),
        ],
        in_specs=[VMEM, VMEM],
        out_specs=[VMEM, VMEM],
        scratch_shapes=[pltpu.VMEM((ROWS, TOK), BF16)],
        compiler_params=pltpu.CompilerParams(vmem_limit_bytes=32 << 20),
        cost_estimate=pl.CostEstimate(flops=3 << 30, bytes_accessed=4 << 20, transcendentals=2 << 20),
        name="diagonal",
    )(q, kv)


ACC = (QH, ROWS, TOK)
SHIFT = (QH, 1, TOK)
SCRATCH = [pltpu.VMEM((HALF, HD), BF16), pltpu.VMEM((ROWS, HALF), BF16), pltpu.SMEM((32,), jnp.int32)]


def halves(refs):
    parts = []
    for ref in refs:
        parts += [ref] if ref.shape[0] == HALF else [ref.at[:HALF], ref.at[HALF:]]
    return parts


def run_units(meta, order, q_refs, q_ids, kv_refs, blocks, accs, shifts, kb, vt, flags):
    kv_refs = halves(kv_refs)
    nq, nb = len(q_ids), len(blocks)
    assert len(kv_refs) == nb
    vt[HD:, :] = jnp.ones((8, HALF), BF16)
    for n, block in enumerate(blocks):
        rank = rank_of(meta, order, *block)
        for q, q_id in enumerate(q_ids):
            flags[n * nq + q] = (rank < order[meta[q_id]]).astype(jnp.int32)

    def one(n):
        some = flags[n * nq]
        for q in range(1, nq):
            some += flags[n * nq + q]

        @pl.when(some > 0)
        def _():
            for place in range(nb):
                @pl.when(n == place)
                def _():
                    kb[...] = kv_refs[place][:, :HD]
                    fill_values(vt, kv_refs[place])

            def query(q):
                @pl.when(flags[n * nq + q] > 0)
                def _():
                    absorb(kb, vt, q_refs.at[q], accs.at[q], shifts.at[q])

            if nq == 1:
                query(0)
            else:
                pl.loop(0, nq)(query)

    if nb == 1:
        one(0)
    else:
        pl.loop(0, nb)(one)


def stage(meta, order, qs, kvs, blocks, states):
    nk = len(kvs)
    first = states[0] is None
    old = list(states[1]) if first else list(states)

    def kernel(*refs):
        meta_ref, order_ref = refs[:2]
        q_refs = refs[2:4]
        kv_refs = refs[4:4 + nk]
        old_acc, old_shift, acc, shift, q_both, kb, vt, flags = refs[4 + nk:]
        for q in range(2):
            q_both[q] = q_refs[q][...]
        if first:
            acc[1] = old_acc[...]
            shift[1] = old_shift[...]
            acc[0] = jnp.zeros(ACC, F32)
            for h in range(QH):
                sample = dot_last(kv_refs[0][:HD, :HD], head(q_refs[0], h))
                shift[0, h] = jnp.max(sample, axis=0, keepdims=True) * SCALE
        else:
            acc[...] = old_acc[...]
            shift[...] = old_shift[...]
        run_units(meta_ref, order_ref, q_both, [2, 0], kv_refs, blocks, acc, shift, kb, vt, flags)

    return pl.pallas_call(
        kernel,
        out_shape=[jax.ShapeDtypeStruct((2,) + ACC, F32), jax.ShapeDtypeStruct((2,) + SHIFT, F32)],
        in_specs=[SMEM, SMEM] + [VMEM] * (4 + nk),
        out_specs=[VMEM, VMEM],
        scratch_shapes=[pltpu.VMEM((2, TOK, QH * HD), BF16)] + SCRATCH,
        compiler_params=pltpu.CompilerParams(vmem_limit_bytes=32 << 20),
        cost_estimate=pl.CostEstimate(
            flops=2 * len(blocks) << 30, bytes_accessed=8 << 20, transcendentals=2 * len(blocks) << 20
        ),
        name="stage",
    )(meta, order, *qs, *kvs, *old)


def recompute(meta, order, q_id, q_ref, sources, acc, shift, kb, vt, buf):
    query_rank = order[meta[q_id]]
    acc[0] = jnp.zeros(ACC, F32)
    shift[0] = jnp.full(SHIFT, -1e30, F32)

    for n, source in enumerate(halves(sources)):
        rank = rank_of(meta, order, n // 8, n // 2 % 4)

        @pl.when(rank <= query_rank)
        def _():
            pltpu.sync_copy(source, buf)
            kb[...] = buf[:, :HD]
            fill_values(vt, buf)

            @pl.loop(0, 16)
            def _(tile):
                h, start = tile & 1, pl.multiple_of((tile >> 1) * HD, HD)
                cols = pl.ds(start, HD)
                keys = lax.broadcasted_iota(jnp.int32, (HALF, HD), 0) + (rank * TOK + n % 2 * HALF)
                rows = lax.broadcasted_iota(jnp.int32, (HALF, HD), 1) + query_rank * TOK + start
                query = q_ref[cols, pl.ds(pl.multiple_of(h * HD, HD), HD)]
                scores = dot_last(kb[...], query) * SCALE
                scores = jnp.where(keys <= rows, scores, -jnp.inf)
                old = shift[0, h, :, cols]
                new = jnp.maximum(old, jnp.max(scores, axis=0, keepdims=True))
                weights = jnp.exp2(scores - new).astype(BF16)
                acc[0, h, :, cols] = acc[0, h, :, cols] * jnp.exp2(old - new) + dot_mid(vt[...], weights)
                shift[0, h, :, cols] = new


def closing(meta, order, q, q_id, kvs, blocks, state, everything, pack):
    nk, ne = len(kvs), len(everything)
    place = 0 if q_id == 2 else 1

    def kernel(*refs):
        meta_ref, order_ref, q_ref = refs[:3]
        kv_refs = refs[3:3 + nk]
        old_acc, old_shift = refs[3 + nk:5 + nk]
        all_refs = refs[5 + nk:5 + nk + ne]
        rest = refs[5 + nk + ne:]
        if pack:
            sent, acc, shift, buf, q_one, kb, vt, flags = rest
        else:
            acc, shift, buf, q_one, kb, vt, flags = rest
        at = place if old_acc.shape[0] == 2 else 0
        acc[0] = old_acc[at]
        shift[0] = old_shift[at]
        q_one[0] = q_ref[...]
        run_units(meta_ref, order_ref, q_one, [q_id], kv_refs, blocks, acc, shift, kb, vt, flags)
        if not ne:
            return
        query_rank = order_ref[meta_ref[q_id]]
        active = jnp.int32(0)
        for n in range(8):
            active += (rank_of(meta_ref, order_ref, n // 4, n % 4) <= query_rank).astype(jnp.int32)
        totals = jnp.concatenate([acc[0, h, HD:HD + 1, :] for h in range(QH)], axis=0)
        fine = jnp.logical_and(totals > 2.0 ** -60, totals < 2.0 ** 100)
        faults = jnp.sum(jnp.where(fine, 0.0, 1.0))

        @pl.when(jnp.logical_and(active > 0, faults > 0.0))
        def _():
            recompute(meta_ref, order_ref, q_id, q_ref, all_refs, acc, shift, kb, vt, buf)

        if pack:
            for h in range(QH):
                total = acc[0, h, HD:HD + 1, :]
                empty = total <= 0.0
                safe = jnp.where(empty, 1.0, total)
                sent[h * HD:(h + 1) * HD, :] = (acc[0, h, :HD, :] * (1.0 / safe)).astype(BF16)
                level = jnp.where(empty, -1e30, shift[0, h] + jnp.log2(safe))
                first = level.astype(BF16).astype(F32)
                second = (level - first).astype(BF16).astype(F32)
                third = level - first - second
                row = lax.broadcasted_iota(jnp.int32, (8, TOK), 0)
                packed = jnp.where(row == 0, first, jnp.where(row == 1, second, third))
                sent[QH * HD + 8 * h:QH * HD + 8 * h + 8, :] = packed.astype(BF16)

    state_shapes = [((1,) + ACC, F32), ((1,) + SHIFT, F32)]
    scratch = [pltpu.VMEM((HALF, 2 * HD), BF16), pltpu.VMEM((1, TOK, QH * HD), BF16)] + SCRATCH
    if pack:
        out_shape = jax.ShapeDtypeStruct((QH * HD + 16, TOK), BF16)
        out_specs = VMEM
        scratch = [pltpu.VMEM(*s) for s in state_shapes] + scratch
    else:
        out_shape = [jax.ShapeDtypeStruct(*s) for s in state_shapes]
        out_specs = [VMEM, VMEM]
    return pl.pallas_call(
        kernel,
        out_shape=out_shape,
        in_specs=[SMEM, SMEM] + [VMEM] * (3 + nk) + [ANY] * ne,
        out_specs=out_specs,
        scratch_shapes=scratch,
        compiler_params=pltpu.CompilerParams(vmem_limit_bytes=32 << 20),
        cost_estimate=pl.CostEstimate(
            flops=len(blocks) << 30, bytes_accessed=8 << 20, transcendentals=len(blocks) << 20
        ),
        name="away" if pack else "home" if ne else "guest",
    )(meta, order, q, *kvs, *state, *everything)


def join_kernel(acc, shift, came, out):
    for h in range(QH):
        total = acc[0, h, HD:HD + 1, :]
        here = shift[0, h] + jnp.log2(total)
        at = QH * HD + 8 * h
        level = came[at:at + 8, :].astype(F32)
        there = level[0:1] + level[1:2] + level[2:3]
        top = jnp.maximum(here, there)
        own, far = jnp.exp2(here - top), jnp.exp2(there - top)
        both = own + far
        mixed = acc[0, h, :HD, :] * (own / (total * both)) + came[h * HD:(h + 1) * HD, :].astype(F32) * (far / both)
        out[:, h * HD:(h + 1) * HD] = mixed.T.astype(BF16)


def join(state, came):
    return pl.pallas_call(
        join_kernel,
        out_shape=jax.ShapeDtypeStruct((TOK, QH * HD), BF16),
        in_specs=[VMEM] * 3,
        out_specs=VMEM,
        compiler_params=pltpu.CompilerParams(vmem_limit_bytes=32 << 20),
        name="join",
    )(*state, came)


def pack_kernel(keys, values, kv, kv_low, kv_high):
    for n in range(TOK // HD):
        tile = slice(n * HD, (n + 1) * HD)
        part = (kv_low, kv_high)[n * HD // HALF]
        at = slice(n * HD % HALF, n * HD % HALF + HD)
        turned = values[tile, :].T
        for out, place in ((kv, tile), (part, at)):
            out[place, :HD] = keys[tile, :]
            out[place, HD:] = turned


def packed_kv(keys, values):
    return pl.pallas_call(
        pack_kernel,
        out_shape=[jax.ShapeDtypeStruct((rows, 2 * HD), BF16) for rows in (TOK, HALF, HALF)],
        in_specs=[VMEM] * 2,
        out_specs=[VMEM] * 3,
        name="pack_kv",
    )(keys, values)


def body(q0, keys, values, order):
    index = lax.axis_index("ctx")
    core = lax.axis_index("head") & 1
    y, z = index >> 2, index & 3
    even, odd = y ^ 1, (((y + 3) & 3 ^ 1) + 1) & 3
    key_y = jnp.where(core == 0, even, odd)
    query_y = jnp.where(core == 0, odd, even)
    meta = jnp.stack([index, key_y * 4 + z, query_y * 4 + z, jnp.where(core == 0, 3, 1)]).astype(jnp.int32)

    key_perm, query_perm = mate_perm(key_mate), mate_perm(query_mate)
    forth, back = ring_perm(1), ring_perm(-1)
    kv, kv_low, kv_high = packed_kv(keys, values)
    a_low, b_low = send(kv_low, forth), send(kv_low, back)
    mate_own = send(kv, key_perm)
    q1 = send(q0, query_perm)
    a_high, b_high = send(kv_high, forth), send(kv_high, back)
    state0 = diagonal(q0, kv)

    far_low = send(a_low, forth)
    mate_a_low, mate_b_low = send(a_low, key_perm), send(b_low, key_perm)
    qs = [q1, q0]
    state = stage(
        meta, order, qs, [kv, mate_own, a_low, b_low],
        [(0, OWN), (0, OWN), (1, OWN), (1, OWN), (0, NEAR_A), (0, NEAR_B)], [None, state0],
    )

    a_high, b_high, shift = lax.optimization_barrier((a_high, b_high, state[1]))
    far_high = send(a_high, forth)
    mate_a_high, mate_b_high = send(a_high, key_perm), send(b_high, key_perm)
    state = stage(
        meta, order, qs, [a_high, b_high, mate_a_low, mate_b_low],
        [(0, NEAR_A), (0, NEAR_B), (1, NEAR_A), (1, NEAR_B)], [state[0], shift],
    )

    far_low, far_high, shift = lax.optimization_barrier((far_low, far_high, state[1]))
    state = [state[0], shift]
    mate_far_low, mate_far_high = send(far_low, key_perm), send(far_high, key_perm)
    late = [mate_a_high, mate_b_high, far_low, far_high]
    late_blocks = [(1, NEAR_A), (1, NEAR_B), (0, FAR), (0, FAR)]
    guest = closing(meta, order, q1, 2, late, late_blocks, state, [], False)
    everything = [
        kv, a_low, a_high, b_low, b_high, far_low, far_high,
        mate_own, mate_a_low, mate_a_high, mate_b_low, mate_b_high, mate_far_low, mate_far_high,
    ]
    last, last_blocks = [mate_far_low, mate_far_high], [(1, FAR), (1, FAR)]
    away = closing(meta, order, q1, 2, last, last_blocks, guest, everything, True)
    came = send(away, query_perm)
    own = closing(meta, order, q0, 0, late + last, late_blocks + last_blocks, state, everything, False)
    return join(own, came)


def solution(mesh):
    in_specs = (P("ctx", "head"), P("ctx", "head"), P("ctx", "head"), P())
    return jax.shard_map(body, mesh=mesh, in_specs=in_specs, out_specs=P("ctx", "head"), check_vma=False)
```

```python
import jax
import jax.numpy as jnp
from jax import lax
from jax.experimental import pallas as pl
from jax.experimental.pallas import tpu as pltpu
from jax.sharding import PartitionSpec as P

HD = 128
QH = 2
TOK = 1024
ROWS = HD + 8
SCALE = 168.0 ** (-0.5) * 1.4426950408889634
VMEM = pl.BlockSpec(memory_space=pltpu.VMEM)
SMEM = pl.BlockSpec(memory_space=pltpu.SMEM)
ANY = pl.BlockSpec(memory_space=pl.ANY)
F32 = jnp.float32
BF16 = jnp.bfloat16


def dot_last(a, b):
    return lax.dot_general(a, b, (((1,), (1,)), ((), ())), preferred_element_type=F32)


def dot_mid(a, b):
    return lax.dot_general(a, b, (((1,), (0,)), ((), ())), preferred_element_type=F32)


def key_mate(y, core):
    return y ^ 1 if core == 0 else (((y - 1) % 4 ^ 1) + 1) % 4


def query_mate(y, core):
    return key_mate(y, 1 - core)


def mate_perm(mate):
    return [
        ((y * 4 + z) * 16 + h, (mate(y, h % 2) * 4 + z) * 16 + h)
        for y in range(4) for z in range(4) for h in range(16)
    ]


def ring_perm(sign):
    return [
        ((y * 4 + z) * 16 + h, (y * 4 + (z + (sign if h // 2 % 2 == 0 else -sign)) % 4) * 16 + h)
        for y in range(4) for z in range(4) for h in range(16)
    ]


def send(array, perm):
    return lax.ppermute(array, ("ctx", "head"), perm)


def head(ref, h):
    return ref[:, h * HD:(h + 1) * HD]


def fill_values(vt, kv_ref):
    for n in range(TOK // HD):
        tile = slice(n * HD, (n + 1) * HD)
        vt[:HD, tile] = kv_ref[tile, HD:]


def absorb(kb, vt, q_ref, acc, shift):
    scores = [dot_last(kb[...], head(q_ref, 0)), None]
    for h in range(QH):
        if h + 1 < QH:
            scores[h + 1] = dot_last(kb[...], head(q_ref, h + 1))
        weights = jnp.exp2(scores[h] * SCALE - shift[h]).astype(BF16)
        acc[h] += dot_mid(vt[...], weights)


OWN, NEAR_A, NEAR_B, FAR = range(4)


def rank_of(meta, order, base, kind):
    index = meta[base]
    offset = (0, meta[3], 4 - meta[3], 2)[kind]
    return order[(index & 12) | ((index + offset) & 3)]


def diagonal_kernel(q_ref, kv_ref, acc, shift, vt):
    vt[HD:, :] = jnp.ones((8, TOK), BF16)
    fill_values(vt, kv_ref)
    keys = lax.broadcasted_iota(jnp.int32, (TOK, TOK), 0)
    rows = lax.broadcasted_iota(jnp.int32, (TOK, TOK), 1)
    for h in range(QH):
        scores = dot_last(kv_ref[:, :HD], head(q_ref, h)) * SCALE
        scores = jnp.where(keys <= rows, scores, -jnp.inf)
        shift[h] = jnp.max(scores, axis=0, keepdims=True)
        weights = jnp.exp2(scores - shift[h]).astype(BF16)
        acc[h] = dot_mid(vt[...], weights)


def diagonal(q, kv):
    return pl.pallas_call(
        diagonal_kernel,
        out_shape=[
            jax.ShapeDtypeStruct((QH, ROWS, TOK), F32),
            jax.ShapeDtypeStruct((QH, 1, TOK), F32),
        ],
        in_specs=[VMEM, VMEM],
        out_specs=[VMEM, VMEM],
        scratch_shapes=[pltpu.VMEM((ROWS, TOK), BF16)],
        compiler_params=pltpu.CompilerParams(vmem_limit_bytes=32 << 20),
        cost_estimate=pl.CostEstimate(flops=3 << 30, bytes_accessed=4 << 20, transcendentals=2 << 20),
        name="diagonal",
    )(q, kv)


ACC = (QH, ROWS, TOK)
SHIFT = (QH, 1, TOK)
SCRATCH = [pltpu.VMEM((TOK, HD), BF16), pltpu.VMEM((ROWS, TOK), BF16), pltpu.SMEM((16,), jnp.int32)]


def run_units(meta, order, q_refs, q_ids, kv_refs, blocks, accs, shifts, kb, vt, flags):
    nq, nb = len(q_ids), len(blocks)
    vt[HD:, :] = jnp.ones((8, TOK), BF16)
    for n, block in enumerate(blocks):
        rank = rank_of(meta, order, *block)
        for q, q_id in enumerate(q_ids):
            flags[n * nq + q] = (rank < order[meta[q_id]]).astype(jnp.int32)

    def one(n):
        some = flags[n * nq]
        for q in range(1, nq):
            some += flags[n * nq + q]

        @pl.when(some > 0)
        def _():
            for place in range(nb):
                @pl.when(n == place)
                def _():
                    kb[...] = kv_refs[place][:, :HD]
                    fill_values(vt, kv_refs[place])

            def query(q):
                @pl.when(flags[n * nq + q] > 0)
                def _():
                    absorb(kb, vt, q_refs.at[q], accs.at[q], shifts.at[q])

            if nq == 1:
                query(0)
            else:
                pl.loop(0, nq)(query)

    if nb == 1:
        one(0)
    else:
        pl.loop(0, nb)(one)


def stage(meta, order, qs, kvs, blocks, states):
    nk = len(kvs)
    first = states[0] is None
    old = list(states[1]) if first else list(states)

    def kernel(*refs):
        meta_ref, order_ref = refs[:2]
        q_refs = refs[2:4]
        kv_refs = refs[4:4 + nk]
        old_acc, old_shift, acc, shift, q_both, kb, vt, flags = refs[4 + nk:]
        for q in range(2):
            q_both[q] = q_refs[q][...]
        if first:
            acc[1] = old_acc[...]
            shift[1] = old_shift[...]
            acc[0] = jnp.zeros(ACC, F32)
            for h in range(QH):
                sample = dot_last(kv_refs[0][:HD, :HD], head(q_refs[0], h))
                shift[0, h] = jnp.max(sample, axis=0, keepdims=True) * SCALE
        else:
            acc[...] = old_acc[...]
            shift[...] = old_shift[...]
        run_units(meta_ref, order_ref, q_both, [2, 0], kv_refs, blocks, acc, shift, kb, vt, flags)

    return pl.pallas_call(
        kernel,
        out_shape=[jax.ShapeDtypeStruct((2,) + ACC, F32), jax.ShapeDtypeStruct((2,) + SHIFT, F32)],
        in_specs=[SMEM, SMEM] + [VMEM] * (4 + nk),
        out_specs=[VMEM, VMEM],
        scratch_shapes=[pltpu.VMEM((2, TOK, QH * HD), BF16)] + SCRATCH,
        compiler_params=pltpu.CompilerParams(vmem_limit_bytes=32 << 20),
        cost_estimate=pl.CostEstimate(
            flops=2 * len(blocks) << 31, bytes_accessed=8 << 20, transcendentals=2 * len(blocks) << 21
        ),
        name="stage",
    )(meta, order, *qs, *kvs, *old)


def recompute(meta, order, q_id, q_ref, sources, acc, shift, buf, kb, vt):
    query_rank = order[meta[q_id]]
    acc[0] = jnp.zeros(ACC, F32)
    shift[0] = jnp.full(SHIFT, -1e30, F32)

    for n, source in enumerate(sources):
        rank = rank_of(meta, order, n // 4, n % 4)

        @pl.when(rank <= query_rank)
        def _():
            pltpu.sync_copy(source, buf)
            kb[...] = buf[:, :HD]
            fill_values(vt, buf)

            @pl.loop(0, 16)
            def _(tile):
                h, start = tile & 1, pl.multiple_of((tile >> 1) * HD, HD)
                cols = pl.ds(start, HD)
                keys = lax.broadcasted_iota(jnp.int32, (TOK, HD), 0) + rank * TOK
                rows = lax.broadcasted_iota(jnp.int32, (TOK, HD), 1) + query_rank * TOK + start
                query = q_ref[cols, pl.ds(pl.multiple_of(h * HD, HD), HD)]
                scores = dot_last(kb[...], query) * SCALE
                scores = jnp.where(keys <= rows, scores, -jnp.inf)
                old = shift[0, h, :, cols]
                new = jnp.maximum(old, jnp.max(scores, axis=0, keepdims=True))
                weights = jnp.exp2(scores - new).astype(BF16)
                acc[0, h, :, cols] = acc[0, h, :, cols] * jnp.exp2(old - new) + dot_mid(vt[...], weights)
                shift[0, h, :, cols] = new


def closing(meta, order, q, q_id, kvs, blocks, state, everything, pack):
    nk, ne = len(kvs), len(everything)
    place = 0 if q_id == 2 else 1

    def kernel(*refs):
        meta_ref, order_ref, q_ref = refs[:3]
        kv_refs = refs[3:3 + nk]
        old_acc, old_shift = refs[3 + nk:5 + nk]
        all_refs = refs[5 + nk:5 + nk + ne]
        rest = refs[5 + nk + ne:]
        if pack:
            sent, acc, shift, buf, q_one, kb, vt, flags = rest
        else:
            acc, shift, buf, q_one, kb, vt, flags = rest
        at = place if old_acc.shape[0] == 2 else 0
        acc[0] = old_acc[at]
        shift[0] = old_shift[at]
        q_one[0] = q_ref[...]
        run_units(meta_ref, order_ref, q_one, [q_id], kv_refs, blocks, acc, shift, kb, vt, flags)
        if not ne:
            return
        query_rank = order_ref[meta_ref[q_id]]
        active = jnp.int32(0)
        for n in range(8):
            active += (rank_of(meta_ref, order_ref, n // 4, n % 4) <= query_rank).astype(jnp.int32)
        totals = jnp.concatenate([acc[0, h, HD:HD + 1, :] for h in range(QH)], axis=0)
        fine = jnp.logical_and(totals > 2.0 ** -60, totals < 2.0 ** 100)
        faults = jnp.sum(jnp.where(fine, 0.0, 1.0))

        @pl.when(jnp.logical_and(active > 0, faults > 0.0))
        def _():
            recompute(meta_ref, order_ref, q_id, q_ref, all_refs, acc, shift, buf, kb, vt)

        if pack:
            for h in range(QH):
                total = acc[0, h, HD:HD + 1, :]
                empty = total <= 0.0
                safe = jnp.where(empty, 1.0, total)
                sent[h * HD:(h + 1) * HD, :] = (acc[0, h, :HD, :] * (1.0 / safe)).astype(BF16)
                level = jnp.where(empty, -1e30, shift[0, h] + jnp.log2(safe))
                first = level.astype(BF16).astype(F32)
                second = (level - first).astype(BF16).astype(F32)
                third = level - first - second
                row = lax.broadcasted_iota(jnp.int32, (8, TOK), 0)
                packed = jnp.where(row == 0, first, jnp.where(row == 1, second, third))
                sent[QH * HD + 8 * h:QH * HD + 8 * h + 8, :] = packed.astype(BF16)

    state_shapes = [((1,) + ACC, F32), ((1,) + SHIFT, F32)]
    scratch = [pltpu.VMEM((TOK, 2 * HD), BF16), pltpu.VMEM((1, TOK, QH * HD), BF16)] + SCRATCH
    if pack:
        out_shape = jax.ShapeDtypeStruct((QH * HD + 16, TOK), BF16)
        out_specs = VMEM
        scratch = [pltpu.VMEM(*s) for s in state_shapes] + scratch
    else:
        out_shape = [jax.ShapeDtypeStruct(*s) for s in state_shapes]
        out_specs = [VMEM, VMEM]
    return pl.pallas_call(
        kernel,
        out_shape=out_shape,
        in_specs=[SMEM, SMEM] + [VMEM] * (3 + nk) + [ANY] * ne,
        out_specs=out_specs,
        scratch_shapes=scratch,
        compiler_params=pltpu.CompilerParams(vmem_limit_bytes=32 << 20),
        cost_estimate=pl.CostEstimate(
            flops=len(blocks) << 31, bytes_accessed=8 << 20, transcendentals=len(blocks) << 21
        ),
        name="away" if pack else "home" if ne else "guest",
    )(meta, order, q, *kvs, *state, *everything)


def join_kernel(acc, shift, came, out):
    for h in range(QH):
        total = acc[0, h, HD:HD + 1, :]
        here = shift[0, h] + jnp.log2(total)
        at = QH * HD + 8 * h
        level = came[at:at + 8, :].astype(F32)
        there = level[0:1] + level[1:2] + level[2:3]
        top = jnp.maximum(here, there)
        own, far = jnp.exp2(here - top), jnp.exp2(there - top)
        both = own + far
        mixed = acc[0, h, :HD, :] * (own / (total * both)) + came[h * HD:(h + 1) * HD, :].astype(F32) * (far / both)
        out[:, h * HD:(h + 1) * HD] = mixed.T.astype(BF16)


def join(state, came):
    return pl.pallas_call(
        join_kernel,
        out_shape=jax.ShapeDtypeStruct((TOK, QH * HD), BF16),
        in_specs=[VMEM] * 3,
        out_specs=VMEM,
        compiler_params=pltpu.CompilerParams(vmem_limit_bytes=32 << 20),
        name="join",
    )(*state, came)


def pack_kernel(keys, values, kv):
    kv[:, :HD] = keys[...]
    for n in range(TOK // HD):
        tile = slice(n * HD, (n + 1) * HD)
        kv[tile, HD:] = values[tile, :].T


def packed_kv(keys, values):
    return pl.pallas_call(
        pack_kernel,
        out_shape=jax.ShapeDtypeStruct((TOK, 2 * HD), BF16),
        in_specs=[VMEM] * 2,
        out_specs=VMEM,
        name="pack_kv",
    )(keys, values)


def body(q0, keys, values, order):
    index = lax.axis_index("ctx")
    place = lax.axis_index("head")
    core, low = place & 1, place >> 1 & 1
    y, z = index >> 2, index & 3
    even, odd = y ^ 1, (((y + 3) & 3 ^ 1) + 1) & 3
    key_y = jnp.where(core == 0, even, odd)
    query_y = jnp.where(core == 0, odd, even)
    meta = jnp.stack([index, key_y * 4 + z, query_y * 4 + z, jnp.where(low == 0, 3, 1)]).astype(jnp.int32)

    key_perm, query_perm = mate_perm(key_mate), mate_perm(query_mate)
    forth, back = ring_perm(1), ring_perm(-1)
    kv = packed_kv(keys, values)
    near_a = send(kv, forth)
    mate_own = send(kv, key_perm)
    q1 = send(q0, query_perm)
    state0 = diagonal(q0, kv)

    kv, near_a = lax.optimization_barrier((kv, near_a))
    near_b = send(kv, back)
    mate_a = send(near_a, key_perm)
    qs = [q1, q0]
    state = stage(
        meta, order, qs, [kv, mate_own, near_a], [(0, OWN), (1, OWN), (0, NEAR_A)], [None, state0]
    )

    near_a, near_b, shift = lax.optimization_barrier((near_a, near_b, state[1]))
    far = send(near_a, forth)
    mate_b = send(near_b, key_perm)
    state = stage(meta, order, qs, [mate_a, near_b], [(1, NEAR_A), (0, NEAR_B)], [state[0], shift])

    far, shift = lax.optimization_barrier((far, state[1]))
    state = [state[0], shift]
    mate_far = send(far, key_perm)
    guest = closing(
        meta, order, q1, 2, [mate_b, far], [(1, NEAR_B), (0, FAR)], state, [], False
    )
    everything = [kv, near_a, near_b, far, mate_own, mate_a, mate_b, mate_far]
    away = closing(meta, order, q1, 2, [mate_far], [(1, FAR)], guest, everything, True)
    came = send(away, query_perm)
    own = closing(
        meta, order, q0, 0, [mate_b, far, mate_far],
        [(1, NEAR_B), (0, FAR), (1, FAR)], state, everything, False,
    )
    return join(own, came)


def solution(mesh):
    in_specs = (P("ctx", "head"), P("ctx", "head"), P("ctx", "head"), P())
    return jax.shard_map(body, mesh=mesh, in_specs=in_specs, out_specs=P("ctx", "head"), check_vma=False)
```

```python
import jax
import jax.numpy as jnp
from jax import lax
from jax.experimental import pallas as pl
from jax.experimental.pallas import tpu as pltpu
from jax.sharding import PartitionSpec as P

HD = 128
QH = 2
TOK = 1024
ROWS = HD + 8
SCALE = 168.0 ** (-0.5) * 1.4426950408889634
VMEM = pl.BlockSpec(memory_space=pltpu.VMEM)
SMEM = pl.BlockSpec(memory_space=pltpu.SMEM)
ANY = pl.BlockSpec(memory_space=pl.ANY)
F32 = jnp.float32
BF16 = jnp.bfloat16


def dot_last(a, b):
    return lax.dot_general(a, b, (((1,), (1,)), ((), ())), preferred_element_type=F32)


def dot_mid(a, b):
    return lax.dot_general(a, b, (((1,), (0,)), ((), ())), preferred_element_type=F32)


def key_mate(y, core):
    return y ^ 1 if core == 0 else (((y - 1) % 4 ^ 1) + 1) % 4


def query_mate(y, core):
    return key_mate(y, 1 - core)


def mate_perm(mate):
    return [
        ((y * 4 + z) * 16 + h, (mate(y, h % 2) * 4 + z) * 16 + h)
        for y in range(4) for z in range(4) for h in range(16)
    ]


def ring_perm(sign):
    return [
        ((y * 4 + z) * 16 + h, (y * 4 + (z + (sign if h // 2 % 2 == 0 else -sign)) % 4) * 16 + h)
        for y in range(4) for z in range(4) for h in range(16)
    ]


def send(array, perm):
    return lax.ppermute(array, ("ctx", "head"), perm)


def head(ref, h):
    return ref[:, h * HD:(h + 1) * HD]


def fill_values(vt, kv_ref):
    for n in range(TOK // HD):
        tile = slice(n * HD, (n + 1) * HD)
        vt[:HD, tile] = kv_ref[tile, HD:]


def absorb(kb, vt, q_ref, acc, shift, heads):
    scores = dot_last(kb[...], head(q_ref, heads[0]))
    for n, h in enumerate(heads):
        upcoming = dot_last(kb[...], head(q_ref, heads[n + 1])) if n + 1 < len(heads) else None
        weights = jnp.exp2(scores * SCALE - shift[h]).astype(BF16)
        acc[h] += dot_mid(vt[...], weights)
        scores = upcoming


OWN, NEAR_A, NEAR_B, FAR = range(4)


def rank_of(meta, order, base, kind):
    index = meta[base]
    offset = (0, meta[3], 4 - meta[3], 2)[kind]
    return order[(index & 12) | ((index + offset) & 3)]


def diagonal_kernel(q_ref, kv_ref, acc, shift, vt):
    vt[HD:, :] = jnp.ones((8, TOK), BF16)
    fill_values(vt, kv_ref)
    keys = lax.broadcasted_iota(jnp.int32, (TOK, TOK), 0)
    rows = lax.broadcasted_iota(jnp.int32, (TOK, TOK), 1)
    for h in range(QH):
        scores = dot_last(kv_ref[:, :HD], head(q_ref, h)) * SCALE
        scores = jnp.where(keys <= rows, scores, -jnp.inf)
        shift[h] = jnp.max(scores, axis=0, keepdims=True)
        weights = jnp.exp2(scores - shift[h]).astype(BF16)
        acc[h] = dot_mid(vt[...], weights)


def diagonal(q, kv):
    return pl.pallas_call(
        diagonal_kernel,
        out_shape=[
            jax.ShapeDtypeStruct((QH, ROWS, TOK), F32),
            jax.ShapeDtypeStruct((QH, 1, TOK), F32),
        ],
        in_specs=[VMEM, VMEM],
        out_specs=[VMEM, VMEM],
        scratch_shapes=[pltpu.VMEM((ROWS, TOK), BF16)],
        compiler_params=pltpu.CompilerParams(vmem_limit_bytes=32 << 20),
        cost_estimate=pl.CostEstimate(flops=3 << 30, bytes_accessed=4 << 20, transcendentals=2 << 20),
        name="diagonal",
    )(q, kv)


ACC = (QH, ROWS, TOK)
SHIFT = (QH, 1, TOK)
SCRATCH = [pltpu.VMEM((TOK, HD), BF16), pltpu.VMEM((ROWS, TOK), BF16), pltpu.SMEM((16,), jnp.int32)]


def run_units(meta, order, q_refs, q_ids, kv_refs, blocks, accs, shifts, kb, vt, flags, heads=(0, 1)):
    nq, nb = len(q_ids), len(blocks)
    vt[HD:, :] = jnp.ones((8, TOK), BF16)
    for n, block in enumerate(blocks):
        rank = rank_of(meta, order, *block)
        for q, q_id in enumerate(q_ids):
            flags[n * nq + q] = (rank < order[meta[q_id]]).astype(jnp.int32)

    def one(n):
        some = flags[n * nq]
        for q in range(1, nq):
            some += flags[n * nq + q]

        @pl.when(some > 0)
        def _():
            for place in range(nb):
                @pl.when(n == place)
                def _():
                    kb[...] = kv_refs[place][:, :HD]
                    fill_values(vt, kv_refs[place])

            def query(q):
                @pl.when(flags[n * nq + q] > 0)
                def _():
                    absorb(kb, vt, q_refs.at[q], accs.at[q], shifts.at[q], heads)

            if nq == 1:
                query(0)
            else:
                pl.loop(0, nq)(query)

    if nb == 1:
        one(0)
    else:
        pl.loop(0, nb)(one)


def stage(meta, order, qs, kvs, blocks, states):
    nk = len(kvs)
    first = states[0] is None
    old = list(states[1]) if first else list(states)

    def kernel(*refs):
        meta_ref, order_ref = refs[:2]
        q_refs = refs[2:4]
        kv_refs = refs[4:4 + nk]
        old_acc, old_shift, acc, shift, q_both, kb, vt, flags = refs[4 + nk:]
        for q in range(2):
            q_both[q] = q_refs[q][...]
        if first:
            acc[1] = old_acc[...]
            shift[1] = old_shift[...]
            acc[0] = jnp.zeros(ACC, F32)
            for h in range(QH):
                sample = dot_last(kv_refs[0][:HD, :HD], head(q_refs[0], h))
                shift[0, h] = jnp.max(sample, axis=0, keepdims=True) * SCALE
        else:
            acc[...] = old_acc[...]
            shift[...] = old_shift[...]
        run_units(meta_ref, order_ref, q_both, [2, 0], kv_refs, blocks, acc, shift, kb, vt, flags)

    return pl.pallas_call(
        kernel,
        out_shape=[jax.ShapeDtypeStruct((2,) + ACC, F32), jax.ShapeDtypeStruct((2,) + SHIFT, F32)],
        in_specs=[SMEM, SMEM] + [VMEM] * (4 + nk),
        out_specs=[VMEM, VMEM],
        scratch_shapes=[pltpu.VMEM((2, TOK, QH * HD), BF16)] + SCRATCH,
        compiler_params=pltpu.CompilerParams(vmem_limit_bytes=32 << 20),
        cost_estimate=pl.CostEstimate(
            flops=2 * len(blocks) << 31, bytes_accessed=8 << 20, transcendentals=2 * len(blocks) << 21
        ),
        name="stage",
    )(meta, order, *qs, *kvs, *old)


def recompute(meta, order, q_id, q_ref, sources, acc, shift, buf, kb, vt):
    query_rank = order[meta[q_id]]
    acc[0] = jnp.zeros(ACC, F32)
    shift[0] = jnp.full(SHIFT, -1e30, F32)

    for n, source in enumerate(sources):
        rank = rank_of(meta, order, n // 4, n % 4)

        @pl.when(rank <= query_rank)
        def _():
            pltpu.sync_copy(source, buf)
            kb[...] = buf[:, :HD]
            fill_values(vt, buf)

            @pl.loop(0, 16)
            def _(tile):
                h, start = tile & 1, pl.multiple_of((tile >> 1) * HD, HD)
                cols = pl.ds(start, HD)
                keys = lax.broadcasted_iota(jnp.int32, (TOK, HD), 0) + rank * TOK
                rows = lax.broadcasted_iota(jnp.int32, (TOK, HD), 1) + query_rank * TOK + start
                query = q_ref[cols, pl.ds(pl.multiple_of(h * HD, HD), HD)]
                scores = dot_last(kb[...], query) * SCALE
                scores = jnp.where(keys <= rows, scores, -jnp.inf)
                old = shift[0, h, :, cols]
                new = jnp.maximum(old, jnp.max(scores, axis=0, keepdims=True))
                weights = jnp.exp2(scores - new).astype(BF16)
                acc[0, h, :, cols] = acc[0, h, :, cols] * jnp.exp2(old - new) + dot_mid(vt[...], weights)
                shift[0, h, :, cols] = new


def closing(meta, order, q, q_id, kvs, blocks, state, everything, pack, heads=(0, 1)):
    nk, ne = len(kvs), len(everything)
    place = 0 if q_id == 2 else 1

    def kernel(*refs):
        meta_ref, order_ref, q_ref = refs[:3]
        kv_refs = refs[3:3 + nk]
        old_acc, old_shift = refs[3 + nk:5 + nk]
        all_refs = refs[5 + nk:5 + nk + ne]
        rest = refs[5 + nk + ne:]
        if pack:
            sent, acc, shift, buf, q_one, kb, vt, flags = rest
        else:
            acc, shift, buf, q_one, kb, vt, flags = rest
        at = place if old_acc.shape[0] == 2 else 0
        for h in heads:
            acc[0, h] = old_acc[at, h]
        shift[0] = old_shift[at]
        q_one[0] = q_ref[...]
        run_units(meta_ref, order_ref, q_one, [q_id], kv_refs, blocks, acc, shift, kb, vt, flags, heads)
        if not ne:
            return
        query_rank = order_ref[meta_ref[q_id]]
        active = jnp.int32(0)
        for n in range(8):
            active += (rank_of(meta_ref, order_ref, n // 4, n % 4) <= query_rank).astype(jnp.int32)
        totals = jnp.concatenate([acc[0, h, HD:HD + 1, :] for h in heads], axis=0)
        fine = jnp.logical_and(totals > 2.0 ** -60, totals < 2.0 ** 100)
        faults = jnp.sum(jnp.where(fine, 0.0, 1.0))

        @pl.when(jnp.logical_and(active > 0, faults > 0.0))
        def _():
            recompute(meta_ref, order_ref, q_id, q_ref, all_refs, acc, shift, buf, kb, vt)

        if pack:
            for n, h in enumerate(heads):
                total = acc[0, h, HD:HD + 1, :]
                empty = total <= 0.0
                safe = jnp.where(empty, 1.0, total)
                sent[n * HD:(n + 1) * HD, :] = (acc[0, h, :HD, :] * (1.0 / safe)).astype(BF16)
                level = jnp.where(empty, -1e30, shift[0, h] + jnp.log2(safe))
                first = level.astype(BF16).astype(F32)
                second = (level - first).astype(BF16).astype(F32)
                third = level - first - second
                row = lax.broadcasted_iota(jnp.int32, (16, TOK), 0)
                packed = jnp.where(row == 0, first, jnp.where(row == 1, second, third))
                sent[len(heads) * HD + 16 * n:len(heads) * HD + 16 * n + 16, :] = packed.astype(BF16)

    state_shapes = [((1,) + ACC, F32), ((1,) + SHIFT, F32)]
    scratch = [pltpu.VMEM((TOK, 2 * HD), BF16), pltpu.VMEM((1, TOK, QH * HD), BF16)] + SCRATCH
    if pack:
        out_shape = jax.ShapeDtypeStruct((len(heads) * (HD + 16), TOK), BF16)
        out_specs = VMEM
        scratch = [pltpu.VMEM(*s) for s in state_shapes] + scratch
    else:
        out_shape = [jax.ShapeDtypeStruct(*s) for s in state_shapes]
        out_specs = [VMEM, VMEM]
    return pl.pallas_call(
        kernel,
        out_shape=out_shape,
        in_specs=[SMEM, SMEM] + [VMEM] * (3 + nk) + [ANY] * ne,
        out_specs=out_specs,
        scratch_shapes=scratch,
        compiler_params=pltpu.CompilerParams(vmem_limit_bytes=32 << 20),
        cost_estimate=pl.CostEstimate(
            flops=len(blocks) << 31, bytes_accessed=8 << 20, transcendentals=len(blocks) << 21
        ),
        name="away" if pack else "home" if ne else "guest",
    )(meta, order, q, *kvs, *state, *everything)


def join_kernel(acc, shift, came_0, came_1, out):
    for h, came in enumerate((came_0, came_1)):
        total = acc[0, h, HD:HD + 1, :]
        here = shift[0, h] + jnp.log2(total)
        level = came[HD:HD + 16, :].astype(F32)
        there = level[0:1] + level[1:2] + level[2:3]
        top = jnp.maximum(here, there)
        own, far = jnp.exp2(here - top), jnp.exp2(there - top)
        both = own + far
        mixed = acc[0, h, :HD, :] * (own / (total * both)) + came[:HD, :].astype(F32) * (far / both)
        out[:, h * HD:(h + 1) * HD] = mixed.T.astype(BF16)


def join(state, came):
    return pl.pallas_call(
        join_kernel,
        out_shape=jax.ShapeDtypeStruct((TOK, QH * HD), BF16),
        in_specs=[VMEM] * 4,
        out_specs=VMEM,
        compiler_params=pltpu.CompilerParams(vmem_limit_bytes=32 << 20),
        name="join",
    )(*state, *came)


def pack_kernel(keys, values, kv):
    kv[:, :HD] = keys[...]
    for n in range(TOK // HD):
        tile = slice(n * HD, (n + 1) * HD)
        kv[tile, HD:] = values[tile, :].T


def packed_kv(keys, values):
    return pl.pallas_call(
        pack_kernel,
        out_shape=jax.ShapeDtypeStruct((TOK, 2 * HD), BF16),
        in_specs=[VMEM] * 2,
        out_specs=VMEM,
        name="pack_kv",
    )(keys, values)


def body(q0, keys, values, order):
    index = lax.axis_index("ctx")
    place = lax.axis_index("head")
    core, low = place & 1, place >> 1 & 1
    y, z = index >> 2, index & 3
    even, odd = y ^ 1, (((y + 3) & 3 ^ 1) + 1) & 3
    key_y = jnp.where(core == 0, even, odd)
    query_y = jnp.where(core == 0, odd, even)
    meta = jnp.stack([index, key_y * 4 + z, query_y * 4 + z, jnp.where(low == 0, 3, 1)]).astype(jnp.int32)

    key_perm, query_perm = mate_perm(key_mate), mate_perm(query_mate)
    forth, back = ring_perm(1), ring_perm(-1)
    kv = packed_kv(keys, values)
    near_a = send(kv, forth)
    mate_own = send(kv, key_perm)
    q1 = send(q0, query_perm)
    state0 = diagonal(q0, kv)

    kv, near_a = lax.optimization_barrier((kv, near_a))
    near_b = send(kv, back)
    mate_a = send(near_a, key_perm)
    qs = [q1, q0]
    state = stage(
        meta, order, qs, [kv, mate_own, near_a], [(0, OWN), (1, OWN), (0, NEAR_A)], [None, state0]
    )

    near_a, near_b, shift = lax.optimization_barrier((near_a, near_b, state[1]))
    far = send(near_a, forth)
    mate_b = send(near_b, key_perm)
    state = stage(meta, order, qs, [mate_a, near_b], [(1, NEAR_A), (0, NEAR_B)], [state[0], shift])

    far, shift = lax.optimization_barrier((far, state[1]))
    state = [state[0], shift]
    mate_far = send(far, key_perm)
    guest = closing(
        meta, order, q1, 2, [mate_b, far], [(1, NEAR_B), (0, FAR)], state, [], False
    )
    everything = [kv, near_a, near_b, far, mate_own, mate_a, mate_b, mate_far]
    came = []
    for h in range(QH):
        away = closing(meta, order, q1, 2, [mate_far], [(1, FAR)], guest, everything, True, (h,))
        came.append(send(away, query_perm))
    own = closing(
        meta, order, q0, 0, [mate_b, far, mate_far],
        [(1, NEAR_B), (0, FAR), (1, FAR)], state, everything, False,
    )
    return join(own, came)


def solution(mesh):
    in_specs = (P("ctx", "head"), P("ctx", "head"), P("ctx", "head"), P())
    return jax.shard_map(body, mesh=mesh, in_specs=in_specs, out_specs=P("ctx", "head"), check_vma=False)
```
